256 devices in a mesh: rows: 8 (over z_lo, x), cols: 32 (over y, z_hi, core).
Axes of the slice: x: 4, y: 4, z: 8 (z_hi: 4, z_lo: 2; z = z_hi * 2 + z_lo), core: 2. Of those that a mesh axis runs over, the one named last changes fastest.
Arguments:
- queries: bfloat16 [65536, 1024], P(('rows', 'cols')), may hold values from -1 to 1
- attn_out: bfloat16 [65536, 1024], P(('rows', 'cols')), may hold values from -6 to 6
- out_grad: bfloat16 [65536, 1024], P(('rows', 'cols')), may hold values from -96 to 96
- log_norm: float32 [65536, 8], P(('rows', 'cols')), may hold values from 7.5 to 8.5
- leaf_kv: bfloat16 [65536, 256], P(('rows', 'cols')), may hold values from -1 to 1
- root_kv: bfloat16 [2048, 256], P('cols'), may hold values from -1 to 1
- branch_kv: bfloat16 [16, 1024, 256], P('rows', 'cols'), may hold values from -1 to 1
- branch_len: int32 [16], replicated, may hold values from 256 to 1024, as said below
- segment_ids: int32 [256, 256], P(('rows', 'cols')), may hold values from 0 to 7, never falling along the last dimension, each value on 1 to 128 neighbouring positions
- segment_branch: int32 [256, 8], P(('rows', 'cols')), may hold values from 0 to 1
Outputs:
- query_grad: bfloat16 [65536, 1024], P(('rows', 'cols'))
- leaf_kv_grad: float32 [65536, 256], P(('rows', 'cols'))
- root_kv_grad: float32 [2048, 256], P('cols')
- branch_kv_grad: float32 [16, 1024, 256], P('rows', 'cols')
The draws below stay inside these ranges and needn't reach their ends.
Inputs may be any that keep to these rules, and one draw needn't show every extreme that they name: `branch_len`: every branch has between 256 and 1024 live slots; some branch has exactly 1024 and some exactly 256. `segment_ids`: never falling along a device's tokens; each segment has 1 to 128 tokens, one exactly 128. `segment_branch`: a segment on row r extends branch r * 2 + value.
All inputs are finite; a program needn't handle non-finite values.
Results may differ from the reference program's by a relative error of at most 0.0041.
Values may be sent and summed in bfloat16 or wider, within the bound.
No kernel may reach another device: no remote copies, remote signals or barrier semaphores. Data moves between devices by JAX's collectives and lax.ppermute only.
A program may use at most 64 MiB of HBM per device.

```python
import math
import jax
import jax.numpy as jnp
import numpy as np
from jax import lax

HEADS = 8
HD = 128
TOK_DEV = 256
ROOT = 2048
BLEN = 1024
BR_DEV = 2
SEGS = 8
SEG_MAX = 128
KVW = 256
BRANCHES = 16
DEVS = 256
LEAF = 65536
N_ROWS = 8
N_COLS = 32


def draw_branch_len(key, part):
    first, second, third = jax.random.split(jax.random.fold_in(key, 71), 3)
    lengths = jax.random.randint(first, (BRANCHES,), BLEN // 4, BLEN + 1, dtype=jnp.int32)
    longest = jax.random.randint(second, (), 0, BRANCHES, dtype=jnp.int32)
    offset = jax.random.randint(third, (), 1, BRANCHES, dtype=jnp.int32)
    shortest = (longest + offset) % BRANCHES
    return lengths.at[longest].set(BLEN).at[shortest].set(BLEN // 4)


def set_ends(values, rng, least, largest):
    longest = values.shape.index(max(values.shape))
    spots = []
    for shift in (0, 1):
        where = [jax.random.randint(jax.random.fold_in(rng, axis), (), 0, length) for axis, length in enumerate(values.shape)]
        where[longest] = (where[longest] + shift) % values.shape[longest]
        spots.append(tuple(where))
    return values.at[spots[0]].set(least).at[spots[1]].set(largest)


def block_scale(stream_key, dims, cuts, low, largest):
    factor_of, own = 1.0, jax.random.fold_in(stream_key, 6)
    for position, blocks in cuts:
        draws = jnp.exp(jax.random.uniform(jax.random.fold_in(own, position), (blocks,), jnp.float32, low / len(cuts), largest / len(cuts)))
        factor_of = factor_of * jnp.repeat(draws, dims[position] // blocks).reshape([-1 if axis == position else 1 for axis in range(len(dims))])
    return factor_of


def profile(amount, total, limit, slope):
    portions = [(1 << 20) // math.isqrt(grade ** slope) + 1 for grade in range(2, amount + 1)]
    rest, counts = total - limit - (amount - 1), [1] * (amount - 1)
    while rest > 0:
        free = [i for i in range(amount - 1) if counts[i] < limit]
        mass, budget = sum([portions[i] for i in free]), rest
        for i in free:
            more = min(limit - counts[i], max(1, budget * portions[i] // mass), rest)
            counts[i] = counts[i] + more
            rest = rest - more
    return np.array([limit] + counts)


def uneven(stream_key, amount, total, reach, slope):
    if amount == 2:
        one = jax.random.randint(stream_key, (), max(1, total - reach), min(reach, total - 1) + 1)
        return jnp.stack([one, total - one])
    sizes = jnp.asarray(profile(amount, total, reach, slope), jnp.int32)
    twos = (amount - 1) // 2
    donor, taker = sizes[1:1 + 2 * twos:2], sizes[2:2 + 2 * twos:2]
    room = jnp.minimum(donor - 1, reach - taker)
    moved = jax.random.randint(jax.random.fold_in(stream_key, 1), (twos,), 0, 1 << 20) % (room + 1)
    sizes = sizes.at[1:1 + 2 * twos:2].set(donor - moved).at[2:2 + 2 * twos:2].set(taker + moved)
    return sizes[jax.random.permutation(jax.random.fold_in(stream_key, 2), amount)]


def centred(own_key, extent, deviation, most, shards=(), kind=jnp.bfloat16):
    drawn = deviation * jax.random.normal(own_key, extent, jnp.float32)
    if shards:
        drawn = drawn * block_scale(own_key, extent, shards, -0.22, 0.18)
    return jnp.clip(drawn, -most, most).astype(kind)


def setup_inputs(seed: int = 0) -> dict:
    streams_of = jax.random.split(jax.random.key(seed), 11)
    return {
        "queries": jnp.clip(jax.random.uniform(streams_of[0], (LEAF, HEADS * HD), jnp.float32, -1.0, 1.0) * block_scale(streams_of[0], (LEAF, HEADS * HD), ((0, 256),), -0.4, 0.0), -1.0, 1.0).astype(jnp.bfloat16),
        "attn_out": centred(streams_of[1], (LEAF, HEADS * HD), 1.0, 6.0, ((0, 256),)),
        "out_grad": centred(streams_of[2], (LEAF, HEADS * HD), 16.0, 96.0, ((0, 256),)),
        "log_norm": jnp.clip(7.5 + 1.0 * jax.random.uniform(streams_of[3], (LEAF, HEADS), jnp.float32) ** block_scale(streams_of[3], (LEAF, HEADS), ((0, 256),), -0.2, 0.2), 7.5, 8.5),
        "leaf_kv": jnp.clip(jax.random.uniform(streams_of[4], (LEAF, KVW), jnp.float32, -1.0, 1.0) * block_scale(streams_of[4], (LEAF, KVW), ((0, 256),), -0.4, 0.0), -1.0, 1.0).astype(jnp.bfloat16),
        "root_kv": jnp.clip(jax.random.uniform(streams_of[5], (ROOT, KVW), jnp.float32, -1.0, 1.0) * block_scale(streams_of[5], (ROOT, KVW), ((0, 32),), -0.4, 0.0), -1.0, 1.0).astype(jnp.bfloat16),
        "branch_kv": jnp.clip(jax.random.uniform(streams_of[6], (BRANCHES, BLEN, KVW), jnp.float32, -1.0, 1.0) * block_scale(streams_of[6], (BRANCHES, BLEN, KVW), ((0, 8), (1, 32)), -0.4, 0.0), -1.0, 1.0).astype(jnp.bfloat16),
        "branch_len": draw_branch_len(jax.random.fold_in(streams_of[10], 71), 0),
        "segment_ids": jax.vmap(lambda own: jnp.searchsorted(jnp.cumsum(uneven(own, SEGS, TOK_DEV, SEG_MAX, 0)), jnp.arange(TOK_DEV), side="right"))(jax.random.split(streams_of[8], DEVS)).reshape((DEVS, TOK_DEV)).astype(jnp.int32),
        "segment_branch": set_ends(jax.random.randint(streams_of[9], (DEVS, SEGS), 0, BR_DEV), jax.random.fold_in(streams_of[9], 1), 0, BR_DEV - 1).astype(jnp.int32),
    }


def block_grads(query_heads, grad_heads, log_norm, row_delta, key_rows, allowed):
    scale = HD ** -0.5
    keys_f = key_rows[:, :HD].astype(jnp.float32)
    values_f = key_rows[:, HD:].astype(jnp.float32)
    query_f = query_heads.astype(jnp.float32)
    grad_f = grad_heads.astype(jnp.float32)
    scores = jnp.einsum('thd,kd->thk', query_f, keys_f) * scale
    weights = jnp.where(allowed[:, None, :], jnp.exp(scores - log_norm[:, :, None]), 0.0)
    dweight = jnp.einsum('thd,kd->thk', grad_f, values_f)
    dscore = weights * (dweight - row_delta[:, :, None])
    weight_b = lax.optimization_barrier(weights.astype(jnp.bfloat16)).astype(jnp.float32)
    dscore_b = lax.optimization_barrier(dscore.astype(jnp.bfloat16)).astype(jnp.float32)
    query_part = jnp.einsum('thk,kd->thd', dscore_b, keys_f) * scale
    key_grad = jnp.einsum('thk,thd->kd', dscore_b, query_f) * scale
    value_grad = jnp.einsum('thk,thd->kd', weight_b, grad_f)
    return query_part, jnp.concatenate([key_grad, value_grad], axis=1)


def device_grads(queries, attn_out, out_grad, log_norm, leaf_kv, segment, seg_branch, root_kv, branch_rows, lengths):
    tokens = queries.shape[0]
    query_heads = queries.reshape(tokens, HEADS, HD)
    grad_heads = out_grad.reshape(tokens, HEADS, HD)
    out_heads = attn_out.reshape(tokens, HEADS, HD)
    row_delta = jnp.sum(grad_heads.astype(jnp.float32) * out_heads.astype(jnp.float32), axis=2)
    full = jnp.ones((tokens, root_kv.shape[0]), dtype=bool)
    query_grad, root_term = block_grads(query_heads, grad_heads, log_norm, row_delta, root_kv, full)
    token_branch = jnp.sum(jnp.where(segment[:, None] == jnp.arange(SEGS, dtype=jnp.int32)[None, :], seg_branch[None, :], 0), axis=1)
    branch_terms = []
    for slot in range(BR_DEV):
        live_slot = jnp.arange(BLEN, dtype=jnp.int32) < lengths[slot]
        allowed = (token_branch == slot)[:, None] & live_slot[None, :]
        part, term = block_grads(query_heads, grad_heads, log_norm, row_delta, branch_rows[slot], allowed)
        query_grad = query_grad + part
        branch_terms.append(term)
    positions = jnp.arange(tokens, dtype=jnp.int32)
    allowed = (segment[:, None] == segment[None, :]) & (positions[None, :] <= positions[:, None])
    part, leaf_term = block_grads(query_heads, grad_heads, log_norm, row_delta, leaf_kv, allowed)
    query_grad = query_grad + part
    return query_grad.reshape(tokens, HEADS * HD).astype(jnp.bfloat16), leaf_term, root_term, jnp.stack(branch_terms)


def reference(queries, attn_out, out_grad, log_norm, leaf_kv, root_kv, branch_kv, branch_len, segment_ids, segment_branch):
    def one_device(carry, device):
        root_acc, branch_acc = carry
        start = device * TOK_DEV

        def rows_of(array):
            return lax.dynamic_slice_in_dim(array, start, TOK_DEV, 0)

        row_start = (device // N_COLS) * BR_DEV
        branch_rows = lax.dynamic_slice_in_dim(branch_kv, row_start, BR_DEV, 0)
        lengths = lax.dynamic_slice_in_dim(branch_len, row_start, BR_DEV, 0)
        segment = lax.dynamic_index_in_dim(segment_ids, device, 0, keepdims=False)
        seg_branch = lax.dynamic_index_in_dim(segment_branch, device, 0, keepdims=False)
        query_grad, leaf_term, root_term, branch_term = device_grads(
            rows_of(queries), rows_of(attn_out), rows_of(out_grad), rows_of(log_norm), rows_of(leaf_kv),
            segment, seg_branch, root_kv, branch_rows, lengths)
        old = lax.dynamic_slice_in_dim(branch_acc, row_start, BR_DEV, 0)
        branch_acc = lax.dynamic_update_slice_in_dim(branch_acc, old + branch_term, row_start, 0)
        return (root_acc + root_term, branch_acc), (query_grad, leaf_term)

    start_carry = (jnp.zeros((ROOT, KVW), jnp.float32), jnp.zeros((BRANCHES, BLEN, KVW), jnp.float32))
    devices = jnp.arange(N_ROWS * N_COLS, dtype=jnp.int32)
    (root_grad, branch_grad), (query_grad, leaf_grad) = lax.scan(one_device, start_carry, devices)
    return (query_grad.reshape(LEAF, HEADS * HD), leaf_grad.reshape(LEAF, KVW), root_grad, branch_grad)
```

```python
import math

import jax
import jax.numpy as jnp
from jax import lax
from jax.experimental import pallas as pl
from jax.experimental.pallas import tpu as pltpu
from jax.sharding import Mesh
from jax.sharding import PartitionSpec as P

HEADS = 8
HD = 128
TOK = 256
SEGS = 8
TILE = 128
TILES = TOK // TILE
TROWS = TILE * HEADS
ROWS = TOK * HEADS
ROOT_SH = 64
BR_SH = 32
NY = 4
NZ = 4
KEYS = NY * NZ * ROOT_SH
BKEYS = NY * NZ * BR_SH
KB = 512
SCALE = HD ** (-0.5)
LOG2E = math.log2(math.e)
BIG = 1e30
BF = jnp.bfloat16
F32 = jnp.float32
VMEM = pl.BlockSpec(memory_space=pltpu.VMEM)
SMEM = pl.BlockSpec(memory_space=pltpu.SMEM)
PARAMS = pltpu.CompilerParams(vmem_limit_bytes=48 << 20)


def dot(a, b, ca, cb):
    return lax.dot_general(a, b, (((ca,), (cb,)), ((), ())), preferred_element_type=F32)


def move(rows, onehot):
    total = None
    for _ in range(3):
        part = rows.astype(BF)
        rows = rows - part.astype(F32)
        term = dot(part, onehot, 1, 1)
        total = term if total is None else total + term
    return total


def pair_terms(keys, values, q, g, norm, delta, mask=None):
    weight = jnp.exp2(dot(keys, q, 1, 1) * (SCALE * LOG2E) - norm)
    if mask is not None:
        weight = jnp.where(mask, weight, 0.0)
    dscore = weight * (dot(values, g, 1, 1) - delta)
    return weight.astype(BF), dscore.astype(BF)


def prepare_kernel(
    seg_branch, q_ref, o_ref, g_ref, norm_ref, leaf_ref, seg_ref, qs_ref, gs_ref, stat_ref, onehot_ref, grad_ref, dq_ref
):
    segment = seg_ref[...]
    lane = lax.broadcasted_iota(jnp.int32, (1, TOK), 1)
    branch = jnp.zeros((1, TOK), jnp.int32)
    first = jnp.zeros((1, TOK), jnp.int32)
    for s in range(SEGS):
        here = segment == s
        branch = jnp.where(here, seg_branch[0, s], branch)
        ahead = jnp.sum((segment < s).astype(F32), axis=1, keepdims=True).astype(jnp.int32)
        first = jnp.where(here, ahead, first)
    zero_branch = (branch == 0).astype(F32)
    row = lax.broadcasted_iota(jnp.int32, (TOK, TOK), 0)
    col = lax.broadcasted_iota(jnp.int32, (TOK, TOK), 1)
    before = (row < col).astype(F32).astype(BF)
    count = dot(jnp.broadcast_to(zero_branch, (8, TOK)).astype(BF), before, 1, 0)[:1].astype(jnp.int32)
    zeros = jnp.sum(zero_branch, axis=1, keepdims=True).astype(jnp.int32)
    rank = jnp.where(branch == 0, count, zeros + lane - count)
    onehot = (row == rank).astype(F32).astype(BF)
    onehot_ref[...] = onehot

    for source, target in ((q_ref, qs_ref), (g_ref, gs_ref)):
        for h in range(HEADS):
            moved = dot(onehot, source[:, h * HD : (h + 1) * HD], 1, 0).astype(BF)
            for t in range(TILES):
                target[pl.ds((t * HEADS + h) * TILE, TILE), :] = moved[t * TILE : (t + 1) * TILE]

    columns = []
    for h in range(HEADS):
        at = slice(h * HD, (h + 1) * HD)
        columns.append(
            jnp.sum(g_ref[:, at].astype(F32) * o_ref[:, at].astype(F32), axis=1, keepdims=True)
        )
    delta = move(jnp.concatenate(columns, axis=1).T, onehot)
    norm = move(norm_ref[...].T, onehot) * LOG2E
    place = jnp.concatenate([lane, first, branch, lane, lane, lane, lane, lane], axis=0)
    place = dot(place.astype(F32).astype(BF), onehot, 1, 1).astype(jnp.int32)
    norm0 = jnp.where(place[2:3] == 0, norm, BIG)
    norm1 = jnp.where(place[2:3] == 0, BIG, norm)
    for t in range(TILES):
        for h in range(HEADS):
            at = pl.ds((t * HEADS + h) * TILE, TILE)
            tok = slice(t * TILE, (t + 1) * TILE)
            for r, value in enumerate((norm, norm0, norm1, delta)):
                stat_ref[r : r + 1, at] = value[h : h + 1, tok]

    keys = leaf_ref[:, :HD]
    values = leaf_ref[:, HD:]
    keys_t = keys.T
    slot = lax.broadcasted_iota(jnp.int32, (TOK, TILE), 0)
    dkey = jnp.zeros((TOK, HD), F32)
    dvalue = jnp.zeros((TOK, HD), F32)
    for t in range(TILES):
        tok = slice(t * TILE, (t + 1) * TILE)
        mask = ((slot >= place[1:2, tok]) & (slot <= place[0:1, tok])).astype(F32)
        mask = jnp.concatenate([mask] * HEADS, axis=1) > 0.0
        at = pl.ds(t * TROWS, TROWS)
        q = qs_ref[at, :]
        g = gs_ref[at, :]
        weight, dscore = pair_terms(keys, values, q, g, stat_ref[0:1, at], stat_ref[3:4, at], mask)
        dkey += dot(dscore, q, 1, 0)
        dvalue += dot(weight, g, 1, 0)
        dq_ref[:, at] = dot(keys_t, dscore, 1, 0)
    grad_ref[:, :HD] = dkey * SCALE
    grad_ref[:, HD:] = dvalue


def sweep(kv_ref, sources, norm_row, grads, base, rows_at):
    keys = kv_ref[rows_at, :HD]
    values = kv_ref[rows_at, HD:]
    keys_t = keys.T
    grads[...] = jnp.zeros_like(grads)
    for q_ref, g_ref, stat_ref, dq_ref in sources:

        def visit(t, carry):
            at = pl.ds(pl.multiple_of(t * TROWS, TROWS), TROWS)
            norm = stat_ref[norm_row : norm_row + 1, at]

            def work():
                q = q_ref[at, :]
                g = g_ref[at, :]
                weight, dscore = pair_terms(keys, values, q, g, norm, stat_ref[3:4, at])
                grads[:, :HD] += dot(dscore, q, 1, 0)
                grads[:, HD:] += dot(weight, g, 1, 0)
                dq_ref[:, at] += dot(keys_t, dscore, 1, 0)

            if norm_row == 0:
                work()
            else:
                pl.when(jnp.min(norm) < 0.5 * BIG)(work)
            return carry

        lax.fori_loop(0, TILES, visit, 0)


def root_kernel(
    kv0, kv1, kv2, kv3, q0, g0, s0, q1, g1, s1, dq_in, dq0, dq1, grad_ref, kv_ref, total
):
    dq0[...] = dq_in[...]
    dq1[...] = jnp.zeros_like(dq1)
    part = KEYS // NY
    for i, piece in enumerate((kv0, kv1, kv2, kv3)):
        kv_ref[pl.ds(i * part, part), :] = piece[...]
    sources = ((q0, g0, s0, dq0), (q1, g1, s1, dq1))

    def block(i, carry):
        at = pl.ds(pl.multiple_of(i * KB, KB), KB)
        sweep(kv_ref, sources, 0, total, 0, at)
        grad_ref[at, :HD] = (total[:, :HD] * SCALE).astype(BF)
        grad_ref[at, HD:] = total[:, HD:].astype(BF)
        return carry

    lax.fori_loop(0, KEYS // KB, block, 0)


def branch_kernel(
    place, lengths, kv0, kv1, kv2, kv3, q0, g0, s0, q1, g1, s1, dq0_in, dq1_in, dq0, dq1, grad_ref, kv_ref, total
):
    dq0[...] = dq0_in[...]
    dq1[...] = dq1_in[...]
    sources = ((q0, g0, s0, dq0), (q1, g1, s1, dq1))
    inner = lax.broadcasted_iota(jnp.int32, (BR_SH, 1), 0)

    def live(b, dy, dz):
        y = lax.rem(place[0] + dy, NY)
        z = lax.rem(place[1] + dz, NZ)
        start = ((y * NZ + z) * 2 + place[2]) * BR_SH
        return inner + start < lengths[b]

    for b in range(2):
        for dy, piece in enumerate((kv0, kv1, kv2, kv3)):
            for dz in range(NZ):
                rows = piece[pl.ds((dz * 2 + b) * BR_SH, BR_SH), :]
                rows = jnp.where(live(b, dy, dz), rows.astype(F32), 0.0).astype(BF)
                kv_ref[pl.ds((dy * NZ + dz) * BR_SH, BR_SH), :] = rows
        sweep(kv_ref, sources, 1 + b, total, 0, pl.ds(0, BKEYS))
        for dy in range(NY):
            for dz in range(NZ):
                at = pl.ds((dy * NZ + dz) * BR_SH, BR_SH)
                to = pl.ds(((dy * NZ + dz) * 2 + b) * BR_SH, BR_SH)
                ok = live(b, dy, dz)
                grad_ref[to, :HD] = jnp.where(ok, total[at, :HD] * SCALE, 0.0).astype(BF)
                grad_ref[to, HD:] = jnp.where(ok, total[at, HD:], 0.0).astype(BF)


def finish_kernel(onehot_ref, mine, other, out_ref):
    for h in range(HEADS):
        parts = []
        for t in range(TILES):
            at = pl.ds((t * HEADS + h) * TILE, TILE)
            parts.append((((mine[:, at] + other[:, at]) * SCALE).T).astype(BF))
        column = jnp.concatenate(parts, axis=0)
        out_ref[:, h * HD : (h + 1) * HD] = dot(onehot_ref[...], column, 0, 0).astype(BF)


def shape(dims, dtype):
    return jax.ShapeDtypeStruct(dims, dtype)


def shift(value, axis, size, by):
    return lax.ppermute(value, axis, [(i, (i + by) % size) for i in range(size)])


def gather(value, axis, size):
    return [value] + [shift(value, axis, size, -k) for k in range(1, size)]


def scatter_sum(blocks, axis, size):
    total = blocks[0].astype(F32)
    for k in range(1, size):
        total = total + shift(blocks[k], axis, size, k).astype(F32)
    return total


def shards(
    queries, attn_out, out_grad, log_norm, leaf_kv, root_kv, branch_kv, branch_len, segment_ids, segment_branch
):
    row_index = lax.axis_index("zl") * 4 + lax.axis_index("x")
    lengths = lax.dynamic_slice_in_dim(branch_len, row_index * 2, 2, 0)
    place = jnp.stack([lax.axis_index("y"), lax.axis_index("zh"), lax.axis_index("c")]).astype(jnp.int32)

    root_z = jnp.concatenate(gather(root_kv, "zh", NZ), axis=0)
    branch_z = jnp.concatenate(gather(branch_kv.reshape(2 * BR_SH, 2 * HD), "zh", NZ), axis=0)
    roots = gather(root_z, "y", NY)
    branches = gather(branch_z, "y", NY)

    q0, g0, s0, onehot, leaf_grad, dq_leaf = pl.pallas_call(
        prepare_kernel,
        out_shape=(
            shape((ROWS, HD), BF),
            shape((ROWS, HD), BF),
            shape((4, ROWS), F32),
            shape((TOK, TOK), BF),
            shape((TOK, 2 * HD), F32),
            shape((HD, ROWS), F32),
        ),
        in_specs=[SMEM] + [VMEM] * 6,
        out_specs=(VMEM,) * 6,
        compiler_params=PARAMS,
        cost_estimate=pl.CostEstimate(flops=4_000_000_000, bytes_accessed=5_000_000, transcendentals=0),
        name="prepare",
    )(segment_branch, queries, attn_out, out_grad, log_norm, leaf_kv, segment_ids)
    q1 = shift(q0, "c", 2, 1)
    g1 = shift(g0, "c", 2, 1)
    s1 = shift(s0, "c", 2, 1)

    dq0, dq1, root_terms = pl.pallas_call(
        root_kernel,
        out_shape=(shape((HD, ROWS), F32), shape((HD, ROWS), F32), shape((KEYS, 2 * HD), BF)),
        in_specs=[VMEM] * 11,
        out_specs=(VMEM,) * 3,
        scratch_shapes=[pltpu.VMEM((KEYS, 2 * HD), BF), pltpu.VMEM((KB, 2 * HD), F32)],
        compiler_params=PARAMS,
        cost_estimate=pl.CostEstimate(flops=10_000_000_000, bytes_accessed=8_000_000, transcendentals=0),
        name="root",
    )(*roots, q0, g0, s0, q1, g1, s1, dq_leaf)

    dq0, dq1, branch_terms = pl.pallas_call(
        branch_kernel,
        out_shape=(shape((HD, ROWS), F32), shape((HD, ROWS), F32), shape((2 * BKEYS, 2 * HD), BF)),
        in_specs=[SMEM] * 2 + [VMEM] * 12,
        out_specs=(VMEM,) * 3,
        scratch_shapes=[pltpu.VMEM((BKEYS, 2 * HD), BF), pltpu.VMEM((BKEYS, 2 * HD), F32)],
        compiler_params=PARAMS,
        cost_estimate=pl.CostEstimate(flops=8_000_000_000, bytes_accessed=8_000_000, transcendentals=0),
        name="branch",
    )(place, lengths, *branches, q0, g0, s0, q1, g1, s1, dq0, dq1)

    root_y = scatter_sum(root_terms.reshape(NY, NZ * ROOT_SH, 2 * HD), "y", NY).astype(BF)
    root_one = scatter_sum(root_y.reshape(NZ, ROOT_SH, 2 * HD), "zh", NZ)
    for axis, size in (("x", 4), ("zl", 2)):
        root_one = root_one + sum(shift(root_one, axis, size, k) for k in range(1, size))

    branch_y = scatter_sum(branch_terms.reshape(NY, NZ * 2 * BR_SH, 2 * HD), "y", NY).astype(BF)
    branch_one = scatter_sum(branch_y.reshape(NZ, 2 * BR_SH, 2 * HD), "zh", NZ)

    query_grad = pl.pallas_call(
        finish_kernel,
        out_shape=shape((TOK, HEADS * HD), BF),
        in_specs=[VMEM] * 3,
        out_specs=VMEM,
        compiler_params=PARAMS,
        cost_estimate=pl.CostEstimate(flops=200_000_000, bytes_accessed=3_000_000, transcendentals=0),
        name="finish",
    )(onehot, dq0, shift(dq1, "c", 2, 1))
    return query_grad, leaf_grad, root_one, branch_one.reshape(2, BR_SH, 2 * HD)


def solution(mesh):
    fine = Mesh(mesh.devices.reshape(2, 4, NY, NZ, 2), ("zl", "x", "y", "zh", "c"))
    rows, cols = ("zl", "x"), ("y", "zh", "c")
    both = rows + cols
    in_specs = (
        P(both, None),
        P(both, None),
        P(both, None),
        P(both, None),
        P(both, None),
        P(cols, None),
        P(rows, cols, None),
        P(),
        P(both, None),
        P(both, None),
    )
    out_specs = (P(both, None), P(both, None), P(cols, None), P(rows, cols, None))
    return jax.shard_map(shards, mesh=fine, in_specs=in_specs, out_specs=out_specs, check_vma=False)
```

```python
import math

import jax
import jax.numpy as jnp
from jax import lax
from jax.experimental import pallas as pl
from jax.experimental.pallas import tpu as pltpu
from jax.sharding import Mesh
from jax.sharding import PartitionSpec as P

HEADS = 8
HD = 128
TOK = 256
SEGS = 8
TILE = 128
TILES = TOK // TILE
TROWS = TILE * HEADS
ROWS = TOK * HEADS
ROOT_SH = 64
BR_SH = 32
NY = 4
NZ = 4
KB = NY * NZ * BR_SH
SCALE = HD ** (-0.5)
LOG2E = math.log2(math.e)
BIG = 1e30
BF = jnp.bfloat16
F32 = jnp.float32
VMEM = pl.BlockSpec(memory_space=pltpu.VMEM)
HBM = pl.BlockSpec(memory_space=pltpu.HBM)
SMEM = pl.BlockSpec(memory_space=pltpu.SMEM)
PARAMS = pltpu.CompilerParams(vmem_limit_bytes=20 << 20)


def dot(a, b, ca, cb):
    return lax.dot_general(a, b, (((ca,), (cb,)), ((), ())), preferred_element_type=F32)


def move(rows, onehot):
    total = None
    for _ in range(3):
        part = rows.astype(BF)
        rows = rows - part.astype(F32)
        term = dot(part, onehot, 1, 1)
        total = term if total is None else total + term
    return total


def pair_terms(keys, values, q, g, norm, delta, mask=None):
    weight = jnp.exp2(dot(keys, q, 1, 1) * (SCALE * LOG2E) - norm)
    if mask is not None:
        weight = jnp.where(mask, weight, 0.0)
    dscore = weight * (dot(values, g, 1, 1) - delta)
    return weight.astype(BF), dscore.astype(BF)


def prepare_kernel(
    seg_branch, q_hbm, o_hbm, g_hbm, norm_ref, leaf_ref, seg_ref, z0, z1, z2, z3,
    qg_ref, stat_ref, onehot_ref, grad_ref, dq_ref, root_ref, branch_ref, q_ref, o_ref, g_ref, sems,
):
    copies = [
        pltpu.make_async_copy(source, target, sems.at[i])
        for i, (source, target) in enumerate(((q_hbm, q_ref), (g_hbm, g_ref), (o_hbm, o_ref)))
    ]
    for copy in copies:
        copy.start()
    for i, piece in enumerate((z0, z1, z2, z3)):
        at = pl.ds(i * ROOT_SH, ROOT_SH)
        root_ref[at, :] = piece[:ROOT_SH, :]
        branch_ref[at, :] = piece[ROOT_SH:, :]
    segment = seg_ref[...]
    lane = lax.broadcasted_iota(jnp.int32, (1, TOK), 1)
    branch = jnp.zeros((1, TOK), jnp.int32)
    first = jnp.zeros((1, TOK), jnp.int32)
    for s in range(SEGS):
        here = segment == s
        branch = jnp.where(here, seg_branch[0, s], branch)
        ahead = jnp.sum((segment < s).astype(F32), axis=1, keepdims=True).astype(jnp.int32)
        first = jnp.where(here, ahead, first)
    zero_branch = (branch == 0).astype(F32)
    row = lax.broadcasted_iota(jnp.int32, (TOK, TOK), 0)
    col = lax.broadcasted_iota(jnp.int32, (TOK, TOK), 1)
    before = (row < col).astype(F32).astype(BF)
    count = dot(jnp.broadcast_to(zero_branch, (8, TOK)).astype(BF), before, 1, 0)[:1].astype(jnp.int32)
    zeros = jnp.sum(zero_branch, axis=1, keepdims=True).astype(jnp.int32)
    rank = jnp.where(branch == 0, count, zeros + lane - count)
    onehot = (row == rank).astype(F32).astype(BF)
    onehot_ref[...] = onehot

    for i, source in enumerate((q_ref, g_ref)):
        copies[i].wait()
        for h in range(HEADS):
            moved = dot(onehot, source[:, h * HD : (h + 1) * HD], 1, 0).astype(BF)
            for t in range(TILES):
                qg_ref[pl.ds(i * ROWS + (t * HEADS + h) * TILE, TILE), :] = moved[t * TILE : (t + 1) * TILE]
    copies[2].wait()

    columns = []
    for h in range(HEADS):
        at = slice(h * HD, (h + 1) * HD)
        columns.append(
            jnp.sum(g_ref[:, at].astype(F32) * o_ref[:, at].astype(F32), axis=1, keepdims=True)
        )
    delta = move(jnp.concatenate(columns, axis=1).T, onehot)
    norm = move(norm_ref[...], onehot) * LOG2E
    place = jnp.concatenate([lane, first, branch, lane, lane, lane, lane, lane], axis=0)
    place = dot(place.astype(F32).astype(BF), onehot, 1, 1).astype(jnp.int32)
    norm0 = jnp.where(place[2:3] == 0, norm, BIG)
    norm1 = jnp.where(place[2:3] == 0, BIG, norm)
    for t in range(TILES):
        for h in range(HEADS):
            at = pl.ds((t * HEADS + h) * TILE, TILE)
            tok = slice(t * TILE, (t + 1) * TILE)
            for r, value in enumerate((norm, norm0, norm1, delta)):
                stat_ref[r : r + 1, at] = value[h : h + 1, tok]

    keys = leaf_ref[:, :HD]
    values = leaf_ref[:, HD:]
    keys_t = keys.T
    slot = lax.broadcasted_iota(jnp.int32, (TOK, TILE), 0)
    dkey = jnp.zeros((TOK, HD), F32)
    dvalue = jnp.zeros((TOK, HD), F32)
    for t in range(TILES):
        tok = slice(t * TILE, (t + 1) * TILE)
        mask = ((slot >= place[1:2, tok]) & (slot <= place[0:1, tok])).astype(F32)
        mask = jnp.concatenate([mask] * HEADS, axis=1) > 0.0
        at = pl.ds(t * TROWS, TROWS)
        q = qg_ref[at, :]
        g = qg_ref[pl.ds(ROWS + t * TROWS, TROWS), :]
        weight, dscore = pair_terms(keys, values, q, g, stat_ref[0:1, at], stat_ref[3:4, at], mask)
        dkey += dot(dscore, q, 1, 0)
        dvalue += dot(weight, g, 1, 0)
        dq_ref[:, at] = dot(keys_t, dscore, 1, 0)
    grad_ref[:, :HD] = dkey * SCALE
    grad_ref[:, HD:] = dvalue


def sweep(kv_ref, sources, norm_row, grads):
    keys = kv_ref[:, :HD]
    values = kv_ref[:, HD:]
    keys_t = keys.T
    grads[...] = jnp.zeros_like(grads)
    for qg_ref, stat_ref, dq_ref in sources:

        def visit(t, carry):
            at = pl.ds(pl.multiple_of(t * TROWS, TROWS), TROWS)
            g_at = pl.ds(pl.multiple_of(ROWS + t * TROWS, TROWS), TROWS)
            norm = stat_ref[norm_row : norm_row + 1, at]

            def work():
                q = qg_ref[at, :]
                g = qg_ref[g_at, :]
                weight, dscore = pair_terms(keys, values, q, g, norm, stat_ref[3:4, at])
                grads[:, :HD] += dot(dscore, q, 1, 0)
                grads[:, HD:] += dot(weight, g, 1, 0)
                dq_ref[:, at] += dot(keys_t, dscore, 1, 0)

            if norm_row == 0:
                work()
            else:
                pl.when(jnp.min(norm) < 0.5 * BIG)(work)
            return carry

        lax.fori_loop(0, TILES, visit, 0)


def root_kernel(kv0, kv1, kv2, kv3, qg0, s0, qg1, s1, dq0, dq1, to0, to1, to2, to3, kv_ref, total):
    dq0[...] = jnp.zeros_like(dq0)
    dq1[...] = jnp.zeros_like(dq1)
    sources = ((qg0, s0, dq0), (qg1, s1, dq1))
    pieces, targets = (kv0, kv1, kv2, kv3), (to0, to1, to2, to3)
    each = NZ * ROOT_SH
    for first in range(0, NY, KB // each):
        for i in range(KB // each):
            kv_ref[pl.ds(i * each, each), :] = pieces[first + i][...]
        sweep(kv_ref, sources, 0, total)
        for i in range(KB // each):
            at = pl.ds(i * each, each)
            targets[first + i][:, :HD] = (total[at, :HD] * SCALE).astype(BF)
            targets[first + i][:, HD:] = total[at, HD:].astype(BF)


def branch_kernel(
    place, lengths, kv0, kv1, kv2, kv3, qg0, s0, qg1, s1, dq0_in, dq1_in, dq0, dq1, to0, to1, to2, to3, kv_ref, total
):
    dq0[...] = dq0_in[...]
    dq1[...] = dq1_in[...]
    sources = ((qg0, s0, dq0), (qg1, s1, dq1))
    pieces, targets = (kv0, kv1, kv2, kv3), (to0, to1, to2, to3)
    inner = lax.broadcasted_iota(jnp.int32, (BR_SH, 1), 0)

    def live(b, dy, dz):
        y = lax.rem(place[0] + dy, NY)
        z = lax.rem(place[1] + dz, NZ)
        return inner + ((y * NZ + z) * 2 + place[2]) * BR_SH < lengths[b]

    for b in range(2):
        for dy in range(NY):
            for z in range(NZ):
                rows = pieces[dy][pl.ds((z * 2 + b) * BR_SH, BR_SH), :].astype(F32)
                at = pl.ds((dy * NZ + z) * BR_SH, BR_SH)
                kv_ref[at, :] = jnp.where(live(b, dy, z), rows, 0.0).astype(BF)
        sweep(kv_ref, sources, 1 + b, total)
        for dy in range(NY):
            for z in range(NZ):
                ok = live(b, dy, z)
                at = pl.ds((dy * NZ + z) * BR_SH, BR_SH)
                to = pl.ds((z * 2 + b) * BR_SH, BR_SH)
                targets[dy][to, :HD] = jnp.where(ok, total[at, :HD] * SCALE, 0.0).astype(BF)
                targets[dy][to, HD:] = jnp.where(ok, total[at, HD:], 0.0).astype(BF)


def finish_kernel(onehot_ref, leaf, mine, other, out_ref):
    for h in range(HEADS):
        parts = []
        for t in range(TILES):
            at = pl.ds((t * HEADS + h) * TILE, TILE)
            parts.append((((leaf[:, at] + mine[:, at] + other[:, at]) * SCALE).T).astype(BF))
        column = jnp.concatenate(parts, axis=0)
        out_ref[:, h * HD : (h + 1) * HD] = dot(onehot_ref[...], column, 0, 0).astype(BF)


def shape(dims, dtype):
    return jax.ShapeDtypeStruct(dims, dtype)


def shift(value, axis, size, by):
    return lax.ppermute(value, axis, [(i, (i + by) % size) for i in range(size)])


def gather(value, axis, size):
    return [value] + [shift(value, axis, size, -k) for k in range(1, size)]


def exchange(blocks, axis, size):
    return [blocks[0]] + [shift(blocks[k], axis, size, k) for k in range(1, size)]


def added(terms):
    return sum(term.astype(F32) for term in terms[1:]) + terms[0].astype(F32)


def shards(
    queries, attn_out, out_grad, log_norm, leaf_kv, root_kv, branch_kv, branch_len, segment_ids, segment_branch
):
    row_index = lax.axis_index("zl") * 4 + lax.axis_index("x")
    lengths = lax.dynamic_slice_in_dim(branch_len, row_index * 2, 2, 0)
    place = jnp.stack([lax.axis_index("y"), lax.axis_index("zh"), lax.axis_index("c")]).astype(jnp.int32)

    shard = jnp.concatenate([root_kv, branch_kv.reshape(2 * BR_SH, 2 * HD)], axis=0)
    block = shape((NZ * ROOT_SH, 2 * HD), BF)
    qg0, s0, onehot, leaf_grad, dq_leaf, root_z, branch_z = pl.pallas_call(
        prepare_kernel,
        out_shape=(
            shape((2 * ROWS, HD), BF),
            shape((4, ROWS), F32),
            shape((TOK, TOK), BF),
            shape((TOK, 2 * HD), F32),
            shape((HD, ROWS), F32),
            block,
            block,
        ),
        in_specs=[SMEM] + [HBM] * 3 + [VMEM] * 7,
        out_specs=(VMEM,) * 7,
        scratch_shapes=[pltpu.VMEM((TOK, HEADS * HD), BF)] * 3 + [pltpu.SemaphoreType.DMA((3,))],
        compiler_params=PARAMS,
        cost_estimate=pl.CostEstimate(flops=4_000_000_000, bytes_accessed=5_000_000, transcendentals=0),
        name="prepare",
    )(segment_branch, *(pltpu.with_memory_space_constraint(x, pltpu.HBM) for x in (queries, attn_out, out_grad)), log_norm.T, leaf_kv, segment_ids, *gather(shard, "zh", NZ))
    roots = gather(root_z, "y", NY)
    branches = gather(branch_z, "y", NY)
    qg1 = shift(qg0, "c", 2, 1)
    s1 = shift(s0, "c", 2, 1)
    tokens = (qg0, s0, qg1, s1)
    dq_shape = shape((HD, ROWS), F32)


    scratch = [pltpu.VMEM((KB, 2 * HD), BF), pltpu.VMEM((KB, 2 * HD), F32)]

    dq0, dq1, *root_terms = pl.pallas_call(
        root_kernel,
        out_shape=(dq_shape, dq_shape, block, block, block, block),
        in_specs=[VMEM] * 8,
        out_specs=(VMEM,) * 6,
        scratch_shapes=scratch,
        compiler_params=PARAMS,
        cost_estimate=pl.CostEstimate(flops=10_000_000_000, bytes_accessed=8_000_000, transcendentals=0),
        name="root",
    )(*roots, *tokens)
    root_y = exchange(root_terms, "y", NY)

    dq0, dq1, *branch_terms = pl.pallas_call(
        branch_kernel,
        out_shape=(dq_shape, dq_shape, block, block, block, block),
        in_specs=[SMEM] * 2 + [VMEM] * 10,
        out_specs=(VMEM,) * 6,
        scratch_shapes=scratch,
        input_output_aliases={10: 0, 11: 1},
        compiler_params=PARAMS,
        cost_estimate=pl.CostEstimate(flops=9_000_000_000, bytes_accessed=8_000_000, transcendentals=0),
        name="branch",
    )(place, lengths, *branches, *tokens, dq0, dq1)
    root_y, branch_terms, dq0, dq1 = lax.optimization_barrier((root_y, branch_terms, dq0, dq1))
    branch_y = exchange(branch_terms, "y", NY)
    root_y = added(root_y).astype(BF).reshape(NZ, ROOT_SH, 2 * HD)
    other, root_y = lax.optimization_barrier((shift(dq1, "c", 2, 1), root_y))
    root_z = [root_y[0]] + [shift(root_y[k], "zh", NZ, k) for k in (1, 2)]
    last, branch_y[1] = lax.optimization_barrier((root_y[3], branch_y[1]))
    root_z.append(shift(last, "zh", NZ, 3))
    query_grad = pl.pallas_call(
        finish_kernel,
        out_shape=shape((TOK, HEADS * HD), BF),
        in_specs=[VMEM] * 4,
        out_specs=VMEM,
        compiler_params=PARAMS,
        cost_estimate=pl.CostEstimate(flops=200_000_000, bytes_accessed=3_000_000, transcendentals=0),
        name="finish",
    )(onehot, dq_leaf, dq0, other)
    branch_y, root_z, query_grad = lax.optimization_barrier((branch_y, root_z, query_grad))

    root_part = added(root_z)
    near = [shift(root_part, "x", 4, k) for k in (1, 2, 3)]
    branch_y = added(branch_y).astype(BF).reshape(NZ, 2, BR_SH, 2 * HD)
    branch_z = exchange([branch_y[k] for k in range(NZ)], "zh", NZ)
    root_x = (root_part + near[1]) + (near[0] + near[2])
    root_one = root_x + shift(root_x, "zl", 2, 1)
    branch_one = added(branch_z)
    return query_grad, leaf_grad, root_one, branch_one


def solution(mesh):
    fine = Mesh(mesh.devices.reshape(2, 4, NY, NZ, 2), ("zl", "x", "y", "zh", "c"))
    rows, cols = ("zl", "x"), ("y", "zh", "c")
    both = rows + cols
    in_specs = (
        P(both, None),
        P(both, None),
        P(both, None),
        P(both, None),
        P(both, None),
        P(cols, None),
        P(rows, cols, None),
        P(),
        P(both, None),
        P(both, None),
    )
    out_specs = (P(both, None), P(both, None), P(cols, None), P(rows, cols, None))
    return jax.shard_map(shards, mesh=fine, in_specs=in_specs, out_specs=out_specs, check_vma=False)
```

```python
import math

import jax
import jax.numpy as jnp
from jax import lax
from jax.experimental import pallas as pl
from jax.experimental.pallas import tpu as pltpu
from jax.sharding import Mesh
from jax.sharding import PartitionSpec as P

HEADS = 8
HD = 128
TOK = 256
SEGS = 8
TILE = 128
TILES = TOK // TILE
TROWS = TILE * HEADS
ROWS = TOK * HEADS
ROOT_SH = 64
BR_SH = 32
NY = 4
NZ = 4
KB = NY * NZ * BR_SH
SCALE = HD ** (-0.5)
LOG2E = math.log2(math.e)
BIG = 1e30
BF = jnp.bfloat16
F32 = jnp.float32
VMEM = pl.BlockSpec(memory_space=pltpu.VMEM)
HBM = pl.BlockSpec(memory_space=pltpu.HBM)
SMEM = pl.BlockSpec(memory_space=pltpu.SMEM)
PARAMS = pltpu.CompilerParams(vmem_limit_bytes=20 << 20)


def dot(a, b, ca, cb):
    return lax.dot_general(a, b, (((ca,), (cb,)), ((), ())), preferred_element_type=F32)


def move(rows, onehot):
    total = None
    for _ in range(3):
        part = rows.astype(BF)
        rows = rows - part.astype(F32)
        term = dot(part, onehot, 1, 1)
        total = term if total is None else total + term
    return total


def pair_terms(keys, values, q, g, norm, delta, mask=None):
    weight = jnp.exp2(dot(keys, q, 1, 1) * (SCALE * LOG2E) - norm)
    if mask is not None:
        weight = jnp.where(mask, weight, 0.0)
    dscore = weight * (dot(values, g, 1, 1) - delta)
    return weight.astype(BF), dscore.astype(BF)


def prepare_kernel(
    seg_branch, q_hbm, o_hbm, g_hbm, norm_ref, leaf_ref, seg_ref,
    qg_ref, stat_ref, onehot_ref, grad_ref, dq_ref, q_ref, o_ref, g_ref, sems,
):
    copies = [
        pltpu.make_async_copy(source, target, sems.at[i])
        for i, (source, target) in enumerate(((q_hbm, q_ref), (g_hbm, g_ref), (o_hbm, o_ref)))
    ]
    for copy in copies:
        copy.start()
    segment = seg_ref[...]
    lane = lax.broadcasted_iota(jnp.int32, (1, TOK), 1)
    branch = jnp.zeros((1, TOK), jnp.int32)
    first = jnp.zeros((1, TOK), jnp.int32)
    for s in range(SEGS):
        here = segment == s
        branch = jnp.where(here, seg_branch[0, s], branch)
        ahead = jnp.sum((segment < s).astype(F32), axis=1, keepdims=True).astype(jnp.int32)
        first = jnp.where(here, ahead, first)
    zero_branch = (branch == 0).astype(F32)
    row = lax.broadcasted_iota(jnp.int32, (TOK, TOK), 0)
    col = lax.broadcasted_iota(jnp.int32, (TOK, TOK), 1)
    before = (row < col).astype(F32).astype(BF)
    count = dot(jnp.broadcast_to(zero_branch, (8, TOK)).astype(BF), before, 1, 0)[:1].astype(jnp.int32)
    zeros = jnp.sum(zero_branch, axis=1, keepdims=True).astype(jnp.int32)
    rank = jnp.where(branch == 0, count, zeros + lane - count)
    onehot = (row == rank).astype(F32).astype(BF)
    onehot_ref[...] = onehot

    for i, source in enumerate((q_ref, g_ref)):
        copies[i].wait()
        for h in range(HEADS):
            moved = dot(onehot, source[:, h * HD : (h + 1) * HD], 1, 0).astype(BF)
            for t in range(TILES):
                qg_ref[pl.ds(i * ROWS + (t * HEADS + h) * TILE, TILE), :] = moved[t * TILE : (t + 1) * TILE]
    copies[2].wait()

    columns = []
    for h in range(HEADS):
        at = slice(h * HD, (h + 1) * HD)
        columns.append(
            jnp.sum(g_ref[:, at].astype(F32) * o_ref[:, at].astype(F32), axis=1, keepdims=True)
        )
    delta = move(jnp.concatenate(columns, axis=1).T, onehot)
    norm = move(norm_ref[...], onehot) * LOG2E
    place = jnp.concatenate([lane, first, branch, lane, lane, lane, lane, lane], axis=0)
    place = dot(place.astype(F32).astype(BF), onehot, 1, 1).astype(jnp.int32)
    norm0 = jnp.where(place[2:3] == 0, norm, BIG)
    norm1 = jnp.where(place[2:3] == 0, BIG, norm)
    for t in range(TILES):
        for h in range(HEADS):
            at = pl.ds((t * HEADS + h) * TILE, TILE)
            tok = slice(t * TILE, (t + 1) * TILE)
            for r, value in enumerate((norm, norm0, norm1, delta)):
                stat_ref[r : r + 1, at] = value[h : h + 1, tok]

    keys = leaf_ref[:, :HD]
    values = leaf_ref[:, HD:]
    keys_t = keys.T
    slot = lax.broadcasted_iota(jnp.int32, (TOK, TILE), 0)
    dkey = jnp.zeros((TOK, HD), F32)
    dvalue = jnp.zeros((TOK, HD), F32)
    for t in range(TILES):
        tok = slice(t * TILE, (t + 1) * TILE)
        mask = ((slot >= place[1:2, tok]) & (slot <= place[0:1, tok])).astype(F32)
        mask = jnp.concatenate([mask] * HEADS, axis=1) > 0.0
        at = pl.ds(t * TROWS, TROWS)
        q = qg_ref[at, :]
        g = qg_ref[pl.ds(ROWS + t * TROWS, TROWS), :]
        weight, dscore = pair_terms(keys, values, q, g, stat_ref[0:1, at], stat_ref[3:4, at], mask)
        dkey += dot(dscore, q, 1, 0)
        dvalue += dot(weight, g, 1, 0)
        dq_ref[:, at] = dot(keys_t, dscore, 1, 0)
    grad_ref[:, :HD] = dkey * SCALE
    grad_ref[:, HD:] = dvalue


def pack_kernel(z0, z1, z2, z3, root_ref, branch_ref):
    for i, piece in enumerate((z0, z1, z2, z3)):
        at = pl.ds(i * ROOT_SH, ROOT_SH)
        root_ref[at, :] = piece[:ROOT_SH, :]
        branch_ref[at, :] = piece[ROOT_SH:, :]


def sweep(kv_ref, sources, norm_row, grads):
    keys = kv_ref[:, :HD]
    values = kv_ref[:, HD:]
    keys_t = keys.T
    for qg_ref, stat_ref, dq_ref in sources:

        def visit(t, carry):
            at = pl.ds(pl.multiple_of(t * TROWS, TROWS), TROWS)
            g_at = pl.ds(pl.multiple_of(ROWS + t * TROWS, TROWS), TROWS)
            norm = stat_ref[norm_row : norm_row + 1, at]

            def work():
                q = qg_ref[at, :]
                g = qg_ref[g_at, :]
                weight, dscore = pair_terms(keys, values, q, g, norm, stat_ref[3:4, at])
                grads[:, :HD] += dot(dscore, q, 1, 0)
                grads[:, HD:] += dot(weight, g, 1, 0)
                dq_ref[:, at] += dot(keys_t, dscore, 1, 0)

            if norm_row == 0:
                work()
            else:
                pl.when(jnp.min(norm) < 0.5 * BIG)(work)
            return carry

        lax.fori_loop(0, TILES, visit, 0)


def root_kernel(kv0, kv1, kv2, kv3, qg0, s0, qg1, s1, dq0, dq1, to0, to1, to2, to3, kv_ref, total):
    dq0[...] = jnp.zeros_like(dq0)
    dq1[...] = jnp.zeros_like(dq1)
    sources = ((qg0, s0, dq0), (qg1, s1, dq1))
    pieces, targets = (kv0, kv1, kv2, kv3), (to0, to1, to2, to3)
    each = NZ * ROOT_SH
    for first in range(0, NY, KB // each):
        for i in range(KB // each):
            kv_ref[pl.ds(i * each, each), :] = pieces[first + i][...]
        total[...] = jnp.zeros_like(total)
        sweep(kv_ref, sources, 0, total)
        for i in range(KB // each):
            at = pl.ds(i * each, each)
            targets[first + i][:, :HD] = (total[at, :HD] * SCALE).astype(BF)
            targets[first + i][:, HD:] = total[at, HD:].astype(BF)


def live_slots(place, lengths, b, dy, dz):
    y = lax.rem(place[0] + dy, NY)
    z = lax.rem(place[1] + dz, NZ)
    start = ((y * NZ + z) * 2 + place[2]) * BR_SH
    return lax.broadcasted_iota(jnp.int32, (BR_SH, 1), 0) + start < lengths[b]


def branch_other_kernel(place, lengths, kv0, kv1, kv2, kv3, qg_ref, stat_ref, dq_in, dq_ref, kv_ref, total):
    dq_ref[...] = dq_in[...]
    total[...] = jnp.zeros_like(total)
    for b in range(2):
        for dy, piece in enumerate((kv0, kv1, kv2, kv3)):
            for dz in range(NZ):
                rows = piece[pl.ds((dz * 2 + b) * BR_SH, BR_SH), :].astype(F32)
                at = pl.ds(b * KB + (dy * NZ + dz) * BR_SH, BR_SH)
                kv_ref[at, :] = jnp.where(live_slots(place, lengths, b, dy, dz), rows, 0.0).astype(BF)
        at = pl.ds(b * KB, KB)
        sweep(kv_ref.at[at, :], ((qg_ref, stat_ref, dq_ref),), 1 + b, total.at[at, :])


def branch_own_kernel(
    place, lengths, kv_ref, total_in, qg_ref, stat_ref, dq_in, dq_ref, to0, to1, to2, to3, total
):
    dq_ref[...] = dq_in[...]
    for b in range(2):
        whole = pl.ds(b * KB, KB)
        total[...] = total_in[whole, :]
        sweep(kv_ref.at[whole, :], ((qg_ref, stat_ref, dq_ref),), 1 + b, total)
        for dy, target in enumerate((to0, to1, to2, to3)):
            for dz in range(NZ):
                ok = live_slots(place, lengths, b, dy, dz)
                at = pl.ds((dy * NZ + dz) * BR_SH, BR_SH)
                to = pl.ds((dz * 2 + b) * BR_SH, BR_SH)
                target[to, :HD] = jnp.where(ok, total[at, :HD] * SCALE, 0.0).astype(BF)
                target[to, HD:] = jnp.where(ok, total[at, HD:], 0.0).astype(BF)


def finish_kernel(onehot_ref, leaf, mine, other, out_ref):
    for h in range(HEADS):
        parts = []
        for t in range(TILES):
            at = pl.ds((t * HEADS + h) * TILE, TILE)
            parts.append((((leaf[:, at] + mine[:, at] + other[:, at]) * SCALE).T).astype(BF))
        column = jnp.concatenate(parts, axis=0)
        out_ref[:, h * HD : (h + 1) * HD] = dot(onehot_ref[...], column, 0, 0).astype(BF)


def shape(dims, dtype):
    return jax.ShapeDtypeStruct(dims, dtype)


def shift(value, axis, size, by):
    return lax.ppermute(value, axis, [(i, (i + by) % size) for i in range(size)])


def gather(value, axis, size):
    return [value] + [shift(value, axis, size, -k) for k in range(1, size)]


def exchange(blocks, axis, size):
    return [blocks[0]] + [shift(blocks[k], axis, size, k) for k in range(1, size)]


def added(terms):
    return sum(term.astype(F32) for term in terms[1:]) + terms[0].astype(F32)


def shards(
    queries, attn_out, out_grad, log_norm, leaf_kv, root_kv, branch_kv, branch_len, segment_ids, segment_branch
):
    row_index = lax.axis_index("zl") * 4 + lax.axis_index("x")
    lengths = lax.dynamic_slice_in_dim(branch_len, row_index * 2, 2, 0)
    place = jnp.stack([lax.axis_index("y"), lax.axis_index("zh"), lax.axis_index("c")]).astype(jnp.int32)

    shard = jnp.concatenate([root_kv, branch_kv.reshape(2 * BR_SH, 2 * HD)], axis=0)
    block = shape((NZ * ROOT_SH, 2 * HD), BF)
    qg0, s0, onehot, leaf_grad, dq_leaf = pl.pallas_call(
        prepare_kernel,
        out_shape=(
            shape((2 * ROWS, HD), BF),
            shape((4, ROWS), F32),
            shape((TOK, TOK), BF),
            shape((TOK, 2 * HD), F32),
            shape((HD, ROWS), F32),
        ),
        in_specs=[SMEM] + [HBM] * 3 + [VMEM] * 3,
        out_specs=(VMEM,) * 5,
        scratch_shapes=[pltpu.VMEM((TOK, HEADS * HD), BF)] * 3 + [pltpu.SemaphoreType.DMA((3,))],
        compiler_params=PARAMS,
        cost_estimate=pl.CostEstimate(flops=4_000_000_000, bytes_accessed=5_000_000, transcendentals=0),
        name="prepare",
    )(segment_branch, *(pltpu.with_memory_space_constraint(x, pltpu.HBM) for x in (queries, attn_out, out_grad)), log_norm.T, leaf_kv, segment_ids)
    pieces, qg0, s0 = lax.optimization_barrier((gather(shard, "zh", NZ), qg0, s0))
    root_z, branch_z = pl.pallas_call(
        pack_kernel,
        out_shape=(block, block),
        in_specs=[VMEM] * 4,
        out_specs=(VMEM,) * 2,
        compiler_params=PARAMS,
        cost_estimate=pl.CostEstimate(flops=0, bytes_accessed=600_000, transcendentals=0),
        name="pack",
    )(*pieces)
    roots = gather(root_z, "y", NY)
    branches = gather(branch_z, "y", NY)
    qg1 = shift(qg0, "c", 2, 1)
    s1 = shift(s0, "c", 2, 1)
    tokens = (qg0, s0, qg1, s1)
    dq_shape = shape((HD, ROWS), F32)


    scratch = [pltpu.VMEM((KB, 2 * HD), BF), pltpu.VMEM((KB, 2 * HD), F32)]

    dq0, dq1, *root_terms = pl.pallas_call(
        root_kernel,
        out_shape=(dq_shape, dq_shape, block, block, block, block),
        in_specs=[VMEM] * 8,
        out_specs=(VMEM,) * 6,
        scratch_shapes=scratch,
        compiler_params=PARAMS,
        cost_estimate=pl.CostEstimate(flops=10_000_000_000, bytes_accessed=8_000_000, transcendentals=0),
        name="root",
    )(*roots, *tokens)
    root_y = exchange(root_terms, "y", NY)

    branch_cost = pl.CostEstimate(flops=4_500_000_000, bytes_accessed=5_000_000, transcendentals=0)
    dq1, branch_kv_all, branch_total = pl.pallas_call(
        branch_other_kernel,
        out_shape=(dq_shape, shape((2 * KB, 2 * HD), BF), shape((2 * KB, 2 * HD), F32)),
        in_specs=[SMEM] * 2 + [VMEM] * 7,
        out_specs=(VMEM,) * 3,
        input_output_aliases={8: 0},
        compiler_params=PARAMS,
        cost_estimate=branch_cost,
        name="branch_other",
    )(place, lengths, *branches, qg1, s1, dq1)
    root_y, dq1, branch_total = lax.optimization_barrier((root_y, dq1, branch_total))
    other = shift(dq1, "c", 2, 1)
    root_y = added(root_y).astype(BF).reshape(NZ, ROOT_SH, 2 * HD)
    root_z = exchange([root_y[k] for k in range(NZ)], "zh", NZ)

    dq0, *branch_terms = pl.pallas_call(
        branch_own_kernel,
        out_shape=(dq_shape, block, block, block, block),
        in_specs=[SMEM] * 2 + [VMEM] * 5,
        out_specs=(VMEM,) * 5,
        scratch_shapes=[pltpu.VMEM((KB, 2 * HD), F32)],
        input_output_aliases={6: 0},
        compiler_params=PARAMS,
        cost_estimate=branch_cost,
        name="branch_own",
    )(place, lengths, branch_kv_all, branch_total, qg0, s0, dq0)
    root_z, other, branch_terms, dq0 = lax.optimization_barrier((root_z, other, branch_terms, dq0))

    branch_y = exchange(branch_terms, "y", NY)
    root_part = added(root_z)
    near = [shift(root_part, "x", 4, k) for k in (1, 2, 3)]
    query_grad = pl.pallas_call(
        finish_kernel,
        out_shape=shape((TOK, HEADS * HD), BF),
        in_specs=[VMEM] * 4,
        out_specs=VMEM,
        compiler_params=PARAMS,
        cost_estimate=pl.CostEstimate(flops=200_000_000, bytes_accessed=3_000_000, transcendentals=0),
        name="finish",
    )(onehot, dq_leaf, dq0, other)
    branch_y, near, query_grad = lax.optimization_barrier((branch_y, near, query_grad))

    branch_y = added(branch_y).astype(BF).reshape(NZ, 2, BR_SH, 2 * HD)
    branch_z = exchange([branch_y[k] for k in range(NZ)], "zh", NZ)
    root_x = (root_part + near[1]) + (near[0] + near[2])
    root_one = root_x + shift(root_x, "zl", 2, 1)
    branch_one = added(branch_z)
    return query_grad, leaf_grad, root_one, branch_one


def solution(mesh):
    fine = Mesh(mesh.devices.reshape(2, 4, NY, NZ, 2), ("zl", "x", "y", "zh", "c"))
    rows, cols = ("zl", "x"), ("y", "zh", "c")
    both = rows + cols
    in_specs = (
        P(both, None),
        P(both, None),
        P(both, None),
        P(both, None),
        P(both, None),
        P(cols, None),
        P(rows, cols, None),
        P(),
        P(both, None),
        P(both, None),
    )
    out_specs = (P(both, None), P(both, None), P(cols, None), P(rows, cols, None))
    return jax.shard_map(shards, mesh=fine, in_specs=in_specs, out_specs=out_specs, check_vma=False)
```

```python
import math

import jax
import jax.numpy as jnp
from jax import lax
from jax.experimental import pallas as pl
from jax.experimental.pallas import tpu as pltpu
from jax.sharding import Mesh
from jax.sharding import PartitionSpec as P

HEADS = 8
HD = 128
TOK = 256
SEGS = 8
TILE = 128
TILES = TOK // TILE
TROWS = TILE * HEADS
ROWS = TOK * HEADS
ROOT_SH = 64
BR_SH = 32
NY = 4
NZ = 4
KB = NY * NZ * BR_SH
SCALE = HD ** (-0.5)
LOG2E = math.log2(math.e)
BIG = 1e30
BF = jnp.bfloat16
F32 = jnp.float32
VMEM = pl.BlockSpec(memory_space=pltpu.VMEM)
HBM = pl.BlockSpec(memory_space=pltpu.HBM)
SMEM = pl.BlockSpec(memory_space=pltpu.SMEM)
PARAMS = pltpu.CompilerParams(vmem_limit_bytes=20 << 20)


def dot(a, b, ca, cb):
    return lax.dot_general(a, b, (((ca,), (cb,)), ((), ())), preferred_element_type=F32)


def move(rows, onehot):
    total = None
    for _ in range(3):
        part = rows.astype(BF)
        rows = rows - part.astype(F32)
        term = dot(part, onehot, 1, 1)
        total = term if total is None else total + term
    return total


def pair_terms(keys, values, q, g, norm, delta, mask=None):
    weight = jnp.exp2(dot(keys, q, 1, 1) * (SCALE * LOG2E) - norm)
    if mask is not None:
        weight = jnp.where(mask, weight, 0.0)
    dscore = weight * (dot(values, g, 1, 1) - delta)
    return weight.astype(BF), dscore.astype(BF)


def prepare_kernel(
    seg_branch, q_hbm, o_hbm, g_hbm, norm_ref, leaf_ref, seg_ref,
    qg_ref, stat_ref, onehot_ref, grad_ref, dq_ref, q_ref, o_ref, g_ref, sems,
):
    copies = [
        pltpu.make_async_copy(source, target, sems.at[i])
        for i, (source, target) in enumerate(((q_hbm, q_ref), (g_hbm, g_ref), (o_hbm, o_ref)))
    ]
    for copy in copies:
        copy.start()
    segment = seg_ref[...]
    lane = lax.broadcasted_iota(jnp.int32, (1, TOK), 1)
    branch = jnp.zeros((1, TOK), jnp.int32)
    first = jnp.zeros((1, TOK), jnp.int32)
    for s in range(SEGS):
        here = segment == s
        branch = jnp.where(here, seg_branch[0, s], branch)
        ahead = jnp.sum((segment < s).astype(F32), axis=1, keepdims=True).astype(jnp.int32)
        first = jnp.where(here, ahead, first)
    zero_branch = (branch == 0).astype(F32)
    row = lax.broadcasted_iota(jnp.int32, (TOK, TOK), 0)
    col = lax.broadcasted_iota(jnp.int32, (TOK, TOK), 1)
    before = (row < col).astype(F32).astype(BF)
    count = dot(jnp.broadcast_to(zero_branch, (8, TOK)).astype(BF), before, 1, 0)[:1].astype(jnp.int32)
    zeros = jnp.sum(zero_branch, axis=1, keepdims=True).astype(jnp.int32)
    rank = jnp.where(branch == 0, count, zeros + lane - count)
    onehot = (row == rank).astype(F32).astype(BF)
    onehot_ref[...] = onehot

    for i, source in enumerate((q_ref, g_ref)):
        copies[i].wait()
        for h in range(HEADS):
            moved = dot(onehot, source[:, h * HD : (h + 1) * HD], 1, 0).astype(BF)
            for t in range(TILES):
                qg_ref[pl.ds(i * ROWS + (t * HEADS + h) * TILE, TILE), :] = moved[t * TILE : (t + 1) * TILE]
    copies[2].wait()

    columns = []
    for h in range(HEADS):
        at = slice(h * HD, (h + 1) * HD)
        columns.append(
            jnp.sum(g_ref[:, at].astype(F32) * o_ref[:, at].astype(F32), axis=1, keepdims=True)
        )
    delta = move(jnp.concatenate(columns, axis=1).T, onehot)
    norm = move(norm_ref[...], onehot) * LOG2E
    place = jnp.concatenate([lane, first, branch, lane, lane, lane, lane, lane], axis=0)
    place = dot(place.astype(F32).astype(BF), onehot, 1, 1).astype(jnp.int32)
    norm0 = jnp.where(place[2:3] == 0, norm, BIG)
    norm1 = jnp.where(place[2:3] == 0, BIG, norm)
    for t in range(TILES):
        for h in range(HEADS):
            at = pl.ds((t * HEADS + h) * TILE, TILE)
            tok = slice(t * TILE, (t + 1) * TILE)
            for r, value in enumerate((norm, norm0, norm1, delta)):
                stat_ref[r : r + 1, at] = value[h : h + 1, tok]

    keys = leaf_ref[:, :HD]
    values = leaf_ref[:, HD:]
    keys_t = keys.T
    slot = lax.broadcasted_iota(jnp.int32, (TOK, TILE), 0)
    dkey = jnp.zeros((TOK, HD), F32)
    dvalue = jnp.zeros((TOK, HD), F32)
    for t in range(TILES):
        tok = slice(t * TILE, (t + 1) * TILE)
        mask = ((slot >= place[1:2, tok]) & (slot <= place[0:1, tok])).astype(F32)
        mask = jnp.concatenate([mask] * HEADS, axis=1) > 0.0
        at = pl.ds(t * TROWS, TROWS)
        q = qg_ref[at, :]
        g = qg_ref[pl.ds(ROWS + t * TROWS, TROWS), :]
        weight, dscore = pair_terms(keys, values, q, g, stat_ref[0:1, at], stat_ref[3:4, at], mask)
        dkey += dot(dscore, q, 1, 0)
        dvalue += dot(weight, g, 1, 0)
        dq_ref[:, at] = dot(keys_t, dscore, 1, 0)
    grad_ref[:, :HD] = dkey * SCALE
    grad_ref[:, HD:] = dvalue


def pack_kernel(z0, z1, z2, z3, root_ref, branch_ref):
    for i, piece in enumerate((z0, z1, z2, z3)):
        at = pl.ds(i * ROOT_SH, ROOT_SH)
        root_ref[at, :] = piece[:ROOT_SH, :]
        branch_ref[at, :] = piece[ROOT_SH:, :]


def sweep(kv_ref, sources, norm_row, grads):
    keys = kv_ref[:, :HD]
    values = kv_ref[:, HD:]
    keys_t = keys.T
    for qg_ref, stat_ref, dq_ref in sources:

        def visit(t, carry):
            at = pl.ds(pl.multiple_of(t * TROWS, TROWS), TROWS)
            g_at = pl.ds(pl.multiple_of(ROWS + t * TROWS, TROWS), TROWS)
            norm = stat_ref[norm_row : norm_row + 1, at]

            def work():
                q = qg_ref[at, :]
                g = qg_ref[g_at, :]
                weight, dscore = pair_terms(keys, values, q, g, norm, stat_ref[3:4, at])
                grads[:, :HD] += dot(dscore, q, 1, 0)
                grads[:, HD:] += dot(weight, g, 1, 0)
                dq_ref[:, at] += dot(keys_t, dscore, 1, 0)

            if norm_row == 0:
                work()
            else:
                pl.when(jnp.min(norm) < 0.5 * BIG)(work)
            return carry

        lax.fori_loop(0, TILES, visit, 0)


def root_kernel(kv0, kv1, kv2, kv3, qg0, s0, qg1, s1, dq0, dq1, to0, to1, to2, to3, kv_ref, total):
    dq0[...] = jnp.zeros_like(dq0)
    dq1[...] = jnp.zeros_like(dq1)
    sources = ((qg0, s0, dq0), (qg1, s1, dq1))
    pieces, targets = (kv0, kv1, kv2, kv3), (to0, to1, to2, to3)
    each = NZ * ROOT_SH
    for dy in range(NY):
        kv_ref[pl.ds(dy * each, each), :] = pieces[dy][...]
    total[...] = jnp.zeros_like(total)
    sweep(kv_ref, sources, 0, total)
    for dy in range(NY):
        at = pl.ds(dy * each, each)
        targets[dy][:, :HD] = (total[at, :HD] * SCALE).astype(BF)
        targets[dy][:, HD:] = total[at, HD:].astype(BF)


def live_slots(place, lengths, b, dy, dz):
    y = lax.rem(place[0] + dy, NY)
    z = lax.rem(place[1] + dz, NZ)
    start = ((y * NZ + z) * 2 + place[2]) * BR_SH
    return lax.broadcasted_iota(jnp.int32, (BR_SH, 1), 0) + start < lengths[b]


def branch_other_kernel(place, lengths, kv0, kv1, kv2, kv3, qg_ref, stat_ref, dq_in, dq_ref, kv_ref, total):
    dq_ref[...] = dq_in[...]
    total[...] = jnp.zeros_like(total)
    for b in range(2):
        for dy, piece in enumerate((kv0, kv1, kv2, kv3)):
            for dz in range(NZ):
                rows = piece[pl.ds((dz * 2 + b) * BR_SH, BR_SH), :].astype(F32)
                at = pl.ds(b * KB + (dy * NZ + dz) * BR_SH, BR_SH)
                kv_ref[at, :] = jnp.where(live_slots(place, lengths, b, dy, dz), rows, 0.0).astype(BF)
        at = pl.ds(b * KB, KB)
        sweep(kv_ref.at[at, :], ((qg_ref, stat_ref, dq_ref),), 1 + b, total.at[at, :])


def branch_own_kernel(
    place, lengths, kv_ref, total_in, qg_ref, stat_ref, dq_in, dq_ref, to0, to1, to2, to3, total
):
    dq_ref[...] = dq_in[...]
    for b in range(2):
        whole = pl.ds(b * KB, KB)
        total[...] = total_in[whole, :]
        sweep(kv_ref.at[whole, :], ((qg_ref, stat_ref, dq_ref),), 1 + b, total)
        for dy, target in enumerate((to0, to1, to2, to3)):
            for dz in range(NZ):
                ok = live_slots(place, lengths, b, dy, dz)
                at = pl.ds((dy * NZ + dz) * BR_SH, BR_SH)
                to = pl.ds((dz * 2 + b) * BR_SH, BR_SH)
                target[to, :HD] = jnp.where(ok, total[at, :HD] * SCALE, 0.0).astype(BF)
                target[to, HD:] = jnp.where(ok, total[at, HD:], 0.0).astype(BF)


def finish_kernel(onehot_ref, leaf, mine, other, out_ref):
    for h in range(HEADS):
        parts = []
        for t in range(TILES):
            at = pl.ds((t * HEADS + h) * TILE, TILE)
            parts.append((((leaf[:, at] + mine[:, at] + other[:, at]) * SCALE).T).astype(BF))
        column = jnp.concatenate(parts, axis=0)
        out_ref[:, h * HD : (h + 1) * HD] = dot(onehot_ref[...], column, 0, 0).astype(BF)


def shape(dims, dtype):
    return jax.ShapeDtypeStruct(dims, dtype)


def shift(value, axis, size, by):
    return lax.ppermute(value, axis, [(i, (i + by) % size) for i in range(size)])


def gather(value, axis, size):
    return [value] + [shift(value, axis, size, -k) for k in range(1, size)]


def exchange(blocks, axis, size):
    return [blocks[0]] + [shift(blocks[k], axis, size, k) for k in range(1, size)]


def added(terms):
    return sum(term.astype(F32) for term in terms[1:]) + terms[0].astype(F32)


def shards(
    queries, attn_out, out_grad, log_norm, leaf_kv, root_kv, branch_kv, branch_len, segment_ids, segment_branch
):
    row_index = lax.axis_index("zl") * 4 + lax.axis_index("x")
    lengths = lax.dynamic_slice_in_dim(branch_len, row_index * 2, 2, 0)
    place = jnp.stack([lax.axis_index("y"), lax.axis_index("zh"), lax.axis_index("c")]).astype(jnp.int32)

    shard = jnp.concatenate([root_kv, branch_kv.reshape(2 * BR_SH, 2 * HD)], axis=0)
    block = shape((NZ * ROOT_SH, 2 * HD), BF)
    qg0, s0, onehot, leaf_grad, dq_leaf = pl.pallas_call(
        prepare_kernel,
        out_shape=(
            shape((2 * ROWS, HD), BF),
            shape((4, ROWS), F32),
            shape((TOK, TOK), BF),
            shape((TOK, 2 * HD), F32),
            shape((HD, ROWS), F32),
        ),
        in_specs=[SMEM] + [HBM] * 3 + [VMEM] * 3,
        out_specs=(VMEM,) * 5,
        scratch_shapes=[pltpu.VMEM((TOK, HEADS * HD), BF)] * 3 + [pltpu.SemaphoreType.DMA((3,))],
        compiler_params=PARAMS,
        cost_estimate=pl.CostEstimate(flops=4_000_000_000, bytes_accessed=5_000_000, transcendentals=0),
        name="prepare",
    )(segment_branch, *(pltpu.with_memory_space_constraint(x, pltpu.HBM) for x in (queries, attn_out, out_grad)), log_norm.T, leaf_kv, segment_ids)
    pieces, qg0, s0 = lax.optimization_barrier((gather(shard, "zh", NZ), qg0, s0))
    root_z, branch_z = pl.pallas_call(
        pack_kernel,
        out_shape=(block, block),
        in_specs=[VMEM] * 4,
        out_specs=(VMEM,) * 2,
        compiler_params=PARAMS,
        cost_estimate=pl.CostEstimate(flops=0, bytes_accessed=600_000, transcendentals=0),
        name="pack",
    )(*pieces)
    roots = gather(root_z, "y", NY)
    branches = gather(branch_z, "y", NY)
    qg1 = shift(qg0, "c", 2, 1)
    s1 = shift(s0, "c", 2, 1)
    tokens = (qg0, s0, qg1, s1)
    dq_shape = shape((HD, ROWS), F32)


    scratch = [pltpu.VMEM((2 * KB, 2 * HD), BF), pltpu.VMEM((2 * KB, 2 * HD), F32)]

    dq0, dq1, *root_terms = pl.pallas_call(
        root_kernel,
        out_shape=(dq_shape, dq_shape, block, block, block, block),
        in_specs=[VMEM] * 8,
        out_specs=(VMEM,) * 6,
        scratch_shapes=scratch,
        compiler_params=PARAMS,
        cost_estimate=pl.CostEstimate(flops=10_000_000_000, bytes_accessed=8_000_000, transcendentals=0),
        name="root",
    )(*roots, *tokens)
    root_y = exchange(root_terms, "y", NY)

    branch_cost = pl.CostEstimate(flops=4_500_000_000, bytes_accessed=5_000_000, transcendentals=0)
    dq1, branch_kv_all, branch_total = pl.pallas_call(
        branch_other_kernel,
        out_shape=(dq_shape, shape((2 * KB, 2 * HD), BF), shape((2 * KB, 2 * HD), F32)),
        in_specs=[SMEM] * 2 + [VMEM] * 7,
        out_specs=(VMEM,) * 3,
        input_output_aliases={8: 0},
        compiler_params=PARAMS,
        cost_estimate=branch_cost,
        name="branch_other",
    )(place, lengths, *branches, qg1, s1, dq1)
    root_y, dq1, branch_total = lax.optimization_barrier((root_y, dq1, branch_total))
    other = shift(dq1, "c", 2, 1)
    root_y = added(root_y).astype(BF).reshape(NZ, ROOT_SH, 2 * HD)
    root_z = exchange([root_y[k] for k in range(NZ)], "zh", NZ)

    dq0, *branch_terms = pl.pallas_call(
        branch_own_kernel,
        out_shape=(dq_shape, block, block, block, block),
        in_specs=[SMEM] * 2 + [VMEM] * 5,
        out_specs=(VMEM,) * 5,
        scratch_shapes=[pltpu.VMEM((KB, 2 * HD), F32)],
        input_output_aliases={6: 0},
        compiler_params=PARAMS,
        cost_estimate=branch_cost,
        name="branch_own",
    )(place, lengths, branch_kv_all, branch_total, qg0, s0, dq0)
    root_z, other, branch_terms, dq0 = lax.optimization_barrier((root_z, other, branch_terms, dq0))

    branch_y = exchange(branch_terms, "y", NY)
    query_grad = pl.pallas_call(
        finish_kernel,
        out_shape=shape((TOK, HEADS * HD), BF),
        in_specs=[VMEM] * 4,
        out_specs=VMEM,
        compiler_params=PARAMS,
        cost_estimate=pl.CostEstimate(flops=200_000_000, bytes_accessed=3_000_000, transcendentals=0),
        name="finish",
    )(onehot, dq_leaf, dq0, other)
    root_part = added(root_z)
    pair = lax.ppermute(root_part, "x", [(0, 1), (1, 0), (2, 3), (3, 2)])
    pair, query_grad = lax.optimization_barrier((pair, query_grad))
    root_part = root_part + pair
    pair = lax.ppermute(root_part, "x", [(0, 3), (3, 0), (1, 2), (2, 1)])
    branch_y = added(branch_y).astype(BF).reshape(NZ, 2, BR_SH, 2 * HD)
    branch_z = exchange([branch_y[k] for k in range(NZ)], "zh", NZ)
    root_part = root_part + pair
    root_one = root_part + shift(root_part, "zl", 2, 1)
    branch_one = added(branch_z)
    return query_grad, leaf_grad, root_one, branch_one


def solution(mesh):
    fine = Mesh(mesh.devices.reshape(2, 4, NY, NZ, 2), ("zl", "x", "y", "zh", "c"))
    rows, cols = ("zl", "x"), ("y", "zh", "c")
    both = rows + cols
    in_specs = (
        P(both, None),
        P(both, None),
        P(both, None),
        P(both, None),
        P(both, None),
        P(cols, None),
        P(rows, cols, None),
        P(),
        P(both, None),
        P(both, None),
    )
    out_specs = (P(both, None), P(both, None), P(cols, None), P(rows, cols, None))
    return jax.shard_map(shards, mesh=fine, in_specs=in_specs, out_specs=out_specs, check_vma=False)
```

```python
import math

import jax
import jax.numpy as jnp
from jax import lax
from jax.experimental import pallas as pl
from jax.experimental.pallas import tpu as pltpu
from jax.sharding import Mesh
from jax.sharding import PartitionSpec as P

HEADS = 8
HD = 128
TOK = 256
SEGS = 8
TILE = 128
TILES = TOK // TILE
TROWS = TILE * HEADS
ROWS = TOK * HEADS
ROOT_SH = 64
BR_SH = 32
NY = 4
NZ = 4
KB = NY * NZ * BR_SH
SCALE = HD ** (-0.5)
LOG2E = math.log2(math.e)
BIG = 1e30
BF = jnp.bfloat16
F32 = jnp.float32
VMEM = pl.BlockSpec(memory_space=pltpu.VMEM)
HBM = pl.BlockSpec(memory_space=pltpu.HBM)
SMEM = pl.BlockSpec(memory_space=pltpu.SMEM)
PARAMS = pltpu.CompilerParams(vmem_limit_bytes=20 << 20)


def dot(a, b, ca, cb):
    return lax.dot_general(a, b, (((ca,), (cb,)), ((), ())), preferred_element_type=F32)


def move(rows, onehot):
    total = None
    for _ in range(3):
        part = rows.astype(BF)
        rows = rows - part.astype(F32)
        term = dot(part, onehot, 1, 1)
        total = term if total is None else total + term
    return total


def pair_terms(keys, values, q, g, norm, delta, mask=None):
    weight = jnp.exp2(dot(keys, q, 1, 1) * (SCALE * LOG2E) - norm)
    if mask is not None:
        weight = jnp.where(mask, weight, 0.0)
    dscore = weight * (dot(values, g, 1, 1) - delta)
    return weight.astype(BF), dscore.astype(BF)


def prepare_kernel(
    seg_branch, q_hbm, o_hbm, g_hbm, norm_ref, leaf_ref, seg_ref,
    qg_ref, stat_ref, onehot_ref, grad_ref, dq_ref, q_ref, o_ref, g_ref, sems,
):
    copies = [
        pltpu.make_async_copy(source, target, sems.at[i])
        for i, (source, target) in enumerate(((q_hbm, q_ref), (g_hbm, g_ref), (o_hbm, o_ref)))
    ]
    for copy in copies:
        copy.start()
    segment = seg_ref[...]
    lane = lax.broadcasted_iota(jnp.int32, (1, TOK), 1)
    branch = jnp.zeros((1, TOK), jnp.int32)
    first = jnp.zeros((1, TOK), jnp.int32)
    for s in range(SEGS):
        here = segment == s
        branch = jnp.where(here, seg_branch[0, s], branch)
        ahead = jnp.sum((segment < s).astype(F32), axis=1, keepdims=True).astype(jnp.int32)
        first = jnp.where(here, ahead, first)
    zero_branch = (branch == 0).astype(F32)
    row = lax.broadcasted_iota(jnp.int32, (TOK, TOK), 0)
    col = lax.broadcasted_iota(jnp.int32, (TOK, TOK), 1)
    before = (row < col).astype(F32).astype(BF)
    count = dot(jnp.broadcast_to(zero_branch, (8, TOK)).astype(BF), before, 1, 0)[:1].astype(jnp.int32)
    zeros = jnp.sum(zero_branch, axis=1, keepdims=True).astype(jnp.int32)
    rank = jnp.where(branch == 0, count, zeros + lane - count)
    onehot = (row == rank).astype(F32).astype(BF)
    onehot_ref[...] = onehot

    for i, source in enumerate((q_ref, g_ref)):
        copies[i].wait()
        for h in range(HEADS):
            moved = dot(onehot, source[:, h * HD : (h + 1) * HD], 1, 0).astype(BF)
            for t in range(TILES):
                qg_ref[pl.ds(i * ROWS + (t * HEADS + h) * TILE, TILE), :] = moved[t * TILE : (t + 1) * TILE]
    copies[2].wait()

    columns = []
    for h in range(HEADS):
        at = slice(h * HD, (h + 1) * HD)
        columns.append(
            jnp.sum(g_ref[:, at].astype(F32) * o_ref[:, at].astype(F32), axis=1, keepdims=True)
        )
    delta = move(jnp.concatenate(columns, axis=1).T, onehot)
    norm = move(norm_ref[...], onehot) * LOG2E
    place = jnp.concatenate([lane, first, branch, lane, lane, lane, lane, lane], axis=0)
    place = dot(place.astype(F32).astype(BF), onehot, 1, 1).astype(jnp.int32)
    norm0 = jnp.where(place[2:3] == 0, norm, BIG)
    norm1 = jnp.where(place[2:3] == 0, BIG, norm)
    for t in range(TILES):
        for h in range(HEADS):
            at = pl.ds((t * HEADS + h) * TILE, TILE)
            tok = slice(t * TILE, (t + 1) * TILE)
            for r, value in enumerate((norm, norm0, norm1, delta)):
                stat_ref[r : r + 1, at] = value[h : h + 1, tok]

    keys = leaf_ref[:, :HD]
    values = leaf_ref[:, HD:]
    keys_t = keys.T
    slot = lax.broadcasted_iota(jnp.int32, (TOK, TILE), 0)
    dkey = jnp.zeros((TOK, HD), F32)
    dvalue = jnp.zeros((TOK, HD), F32)
    for t in range(TILES):
        tok = slice(t * TILE, (t + 1) * TILE)
        mask = ((slot >= place[1:2, tok]) & (slot <= place[0:1, tok])).astype(F32)
        mask = jnp.concatenate([mask] * HEADS, axis=1) > 0.0
        at = pl.ds(t * TROWS, TROWS)
        q = qg_ref[at, :]
        g = qg_ref[pl.ds(ROWS + t * TROWS, TROWS), :]
        weight, dscore = pair_terms(keys, values, q, g, stat_ref[0:1, at], stat_ref[3:4, at], mask)
        dkey += dot(dscore, q, 1, 0)
        dvalue += dot(weight, g, 1, 0)
        dq_ref[:, at] = dot(keys_t, dscore, 1, 0)
    grad_ref[:, :HD] = dkey * SCALE
    grad_ref[:, HD:] = dvalue


def pack_kernel(z0, z1, z2, z3, root_ref, branch_ref):
    for i, piece in enumerate((z0, z1, z2, z3)):
        at = pl.ds(i * ROOT_SH, ROOT_SH)
        root_ref[at, :] = piece[:ROOT_SH, :]
        branch_ref[at, :] = piece[ROOT_SH:, :]


def sweep(kv_ref, sources, norm_row, grads):
    keys = kv_ref[:, :HD]
    values = kv_ref[:, HD:]
    keys_t = keys.T
    for qg_ref, stat_ref, dq_ref in sources:

        def visit(t, carry):
            at = pl.ds(pl.multiple_of(t * TROWS, TROWS), TROWS)
            g_at = pl.ds(pl.multiple_of(ROWS + t * TROWS, TROWS), TROWS)
            norm = stat_ref[norm_row : norm_row + 1, at]

            def work():
                q = qg_ref[at, :]
                g = qg_ref[g_at, :]
                weight, dscore = pair_terms(keys, values, q, g, norm, stat_ref[3:4, at])
                grads[:, :HD] += dot(dscore, q, 1, 0)
                grads[:, HD:] += dot(weight, g, 1, 0)
                dq_ref[:, at] += dot(keys_t, dscore, 1, 0)

            if norm_row == 0:
                work()
            else:
                pl.when(jnp.min(norm) < 0.5 * BIG)(work)
            return carry

        lax.fori_loop(0, TILES, visit, 0)


def root_kernel(kv0, kv1, kv2, kv3, qg0, s0, qg1, s1, dq0, dq1, to0, to1, to2, to3, kv_ref, total):
    dq0[...] = jnp.zeros_like(dq0)
    dq1[...] = jnp.zeros_like(dq1)
    sources = ((qg0, s0, dq0), (qg1, s1, dq1))
    pieces, targets = (kv0, kv1, kv2, kv3), (to0, to1, to2, to3)
    each = NZ * ROOT_SH
    for dy in range(NY):
        kv_ref[pl.ds(dy * each, each), :] = pieces[dy][...]
    total[...] = jnp.zeros_like(total)
    sweep(kv_ref, sources, 0, total)
    for dy in range(NY):
        at = pl.ds(dy * each, each)
        targets[dy][:, :HD] = (total[at, :HD] * SCALE).astype(BF)
        targets[dy][:, HD:] = total[at, HD:].astype(BF)


def live_slots(place, lengths, b, dy, dz):
    y = lax.rem(place[0] + dy, NY)
    z = lax.rem(place[1] + dz, NZ)
    start = ((y * NZ + z) * 2 + place[2]) * BR_SH
    return lax.broadcasted_iota(jnp.int32, (BR_SH, 1), 0) + start < lengths[place[3] + b]


def branch_other_kernel(place, lengths, kv0, kv1, kv2, kv3, qg_ref, stat_ref, dq_in, dq_ref, kv_ref, total):
    dq_ref[...] = dq_in[...]
    total[...] = jnp.zeros_like(total)
    for b in range(2):
        for dy, piece in enumerate((kv0, kv1, kv2, kv3)):
            for dz in range(NZ):
                rows = piece[pl.ds((dz * 2 + b) * BR_SH, BR_SH), :].astype(F32)
                at = pl.ds(b * KB + (dy * NZ + dz) * BR_SH, BR_SH)
                kv_ref[at, :] = jnp.where(live_slots(place, lengths, b, dy, dz), rows, 0.0).astype(BF)
        at = pl.ds(b * KB, KB)
        sweep(kv_ref.at[at, :], ((qg_ref, stat_ref, dq_ref),), 1 + b, total.at[at, :])


def branch_own_kernel(
    place, lengths, kv_ref, total_in, qg_ref, stat_ref, dq_in, dq_ref, to0, to1, to2, to3, total
):
    dq_ref[...] = dq_in[...]
    for b in range(2):
        whole = pl.ds(b * KB, KB)
        total[...] = total_in[whole, :]
        sweep(kv_ref.at[whole, :], ((qg_ref, stat_ref, dq_ref),), 1 + b, total)
        for dy, target in enumerate((to0, to1, to2, to3)):
            for dz in range(NZ):
                ok = live_slots(place, lengths, b, dy, dz)
                at = pl.ds((dy * NZ + dz) * BR_SH, BR_SH)
                to = pl.ds((dz * 2 + b) * BR_SH, BR_SH)
                target[to, :HD] = jnp.where(ok, total[at, :HD] * SCALE, 0.0).astype(BF)
                target[to, HD:] = jnp.where(ok, total[at, HD:], 0.0).astype(BF)


def finish_kernel(onehot_ref, leaf, mine, other, out_ref):
    for h in range(HEADS):
        parts = []
        for t in range(TILES):
            at = pl.ds((t * HEADS + h) * TILE, TILE)
            parts.append((((leaf[:, at] + mine[:, at] + other[:, at]) * SCALE).T).astype(BF))
        column = jnp.concatenate(parts, axis=0)
        out_ref[:, h * HD : (h + 1) * HD] = dot(onehot_ref[...], column, 0, 0).astype(BF)


def shape(dims, dtype):
    return jax.ShapeDtypeStruct(dims, dtype)


def shift(value, axis, size, by):
    return lax.ppermute(value, axis, [(i, (i + by) % size) for i in range(size)])


def gather(value, axis, size):
    return [value] + [shift(value, axis, size, -k) for k in range(1, size)]


def exchange(blocks, axis, size):
    return [blocks[0]] + [shift(blocks[k], axis, size, k) for k in (2, 1, 3)]


def added(terms):
    return sum(term.astype(F32) for term in terms[1:]) + terms[0].astype(F32)


def shards(
    queries, attn_out, out_grad, log_norm, leaf_kv, root_kv, branch_kv, branch_len, segment_ids, segment_branch
):
    first_branch = (lax.axis_index("zl") * 4 + lax.axis_index("x")) * 2
    place = jnp.stack([lax.axis_index("y"), lax.axis_index("zh"), lax.axis_index("c"), first_branch]).astype(jnp.int32)

    shard = jnp.concatenate([root_kv, branch_kv.reshape(2 * BR_SH, 2 * HD)], axis=0)
    block = shape((NZ * ROOT_SH, 2 * HD), BF)
    qg0, s0, onehot, leaf_grad, dq_leaf = pl.pallas_call(
        prepare_kernel,
        out_shape=(
            shape((2 * ROWS, HD), BF),
            shape((4, ROWS), F32),
            shape((TOK, TOK), BF),
            shape((TOK, 2 * HD), F32),
            shape((HD, ROWS), F32),
        ),
        in_specs=[SMEM] + [HBM] * 3 + [VMEM] * 3,
        out_specs=(VMEM,) * 5,
        scratch_shapes=[pltpu.VMEM((TOK, HEADS * HD), BF)] * 3 + [pltpu.SemaphoreType.DMA((3,))],
        compiler_params=PARAMS,
        cost_estimate=pl.CostEstimate(flops=4_000_000_000, bytes_accessed=5_000_000, transcendentals=0),
        name="prepare",
    )(segment_branch, *(pltpu.with_memory_space_constraint(x, pltpu.HBM) for x in (queries, attn_out, out_grad)), log_norm.T, leaf_kv, segment_ids)
    pieces, qg0, s0 = lax.optimization_barrier((gather(shard, "zh", NZ), qg0, s0))
    root_z, branch_z = pl.pallas_call(
        pack_kernel,
        out_shape=(block, block),
        in_specs=[VMEM] * 4,
        out_specs=(VMEM,) * 2,
        compiler_params=PARAMS,
        cost_estimate=pl.CostEstimate(flops=0, bytes_accessed=600_000, transcendentals=0),
        name="pack",
    )(*pieces)
    roots = gather(root_z, "y", NY)
    branches = gather(branch_z, "y", NY)
    qg1 = shift(qg0, "c", 2, 1)
    s1 = shift(s0, "c", 2, 1)
    tokens = (qg0, s0, qg1, s1)
    dq_shape = shape((HD, ROWS), F32)


    scratch = [pltpu.VMEM((2 * KB, 2 * HD), BF), pltpu.VMEM((2 * KB, 2 * HD), F32)]

    dq0, dq1, *root_terms = pl.pallas_call(
        root_kernel,
        out_shape=(dq_shape, dq_shape, block, block, block, block),
        in_specs=[VMEM] * 8,
        out_specs=(VMEM,) * 6,
        scratch_shapes=scratch,
        compiler_params=PARAMS,
        cost_estimate=pl.CostEstimate(flops=10_000_000_000, bytes_accessed=8_000_000, transcendentals=0),
        name="root",
    )(*roots, *tokens)
    root_y = exchange(root_terms, "y", NY)

    branch_cost = pl.CostEstimate(flops=4_500_000_000, bytes_accessed=5_000_000, transcendentals=0)
    dq1, branch_kv_all, branch_total = pl.pallas_call(
        branch_other_kernel,
        out_shape=(dq_shape, shape((2 * KB, 2 * HD), BF), shape((2 * KB, 2 * HD), F32)),
        in_specs=[SMEM] * 2 + [VMEM] * 7,
        out_specs=(VMEM,) * 3,
        input_output_aliases={8: 0},
        compiler_params=PARAMS,
        cost_estimate=branch_cost,
        name="branch_other",
    )(place, branch_len, *branches, qg1, s1, dq1)
    root_y, dq1, branch_total = lax.optimization_barrier((root_y, dq1, branch_total))
    other = shift(dq1, "c", 2, 1)
    root_y = added(root_y).astype(BF).reshape(NZ, ROOT_SH, 2 * HD)
    root_z = exchange([root_y[k] for k in range(NZ)], "zh", NZ)

    dq0, *branch_terms = pl.pallas_call(
        branch_own_kernel,
        out_shape=(dq_shape, block, block, block, block),
        in_specs=[SMEM] * 2 + [VMEM] * 5,
        out_specs=(VMEM,) * 5,
        scratch_shapes=[pltpu.VMEM((KB, 2 * HD), F32)],
        input_output_aliases={6: 0},
        compiler_params=PARAMS,
        cost_estimate=branch_cost,
        name="branch_own",
    )(place, branch_len, branch_kv_all, branch_total, qg0, s0, dq0)
    root_z, other, branch_terms, dq0 = lax.optimization_barrier((root_z, other, branch_terms, dq0))

    branch_y = exchange(branch_terms, "y", NY)
    query_grad = pl.pallas_call(
        finish_kernel,
        out_shape=shape((TOK, HEADS * HD), BF),
        in_specs=[VMEM] * 4,
        out_specs=VMEM,
        compiler_params=PARAMS,
        cost_estimate=pl.CostEstimate(flops=200_000_000, bytes_accessed=3_000_000, transcendentals=0),
        name="finish",
    )(onehot, dq_leaf, dq0, other)
    root_part = added(root_z)
    pair = lax.ppermute(root_part, "x", [(0, 1), (1, 0), (2, 3), (3, 2)])
    pair, query_grad = lax.optimization_barrier((pair, query_grad))
    root_part = root_part + pair
    pair = lax.ppermute(root_part, "x", [(0, 3), (3, 0), (1, 2), (2, 1)])
    branch_y = added(branch_y).astype(BF).reshape(NZ, 2, BR_SH, 2 * HD)
    branch_z = exchange([branch_y[k] for k in range(NZ)], "zh", NZ)
    root_part = root_part + pair
    root_one = root_part + shift(root_part, "zl", 2, 1)
    branch_one = added(branch_z)
    return query_grad, leaf_grad, root_one, branch_one


def solution(mesh):
    fine = Mesh(mesh.devices.reshape(2, 4, NY, NZ, 2), ("zl", "x", "y", "zh", "c"))
    rows, cols = ("zl", "x"), ("y", "zh", "c")
    both = rows + cols
    in_specs = (
        P(both, None),
        P(both, None),
        P(both, None),
        P(both, None),
        P(both, None),
        P(cols, None),
        P(rows, cols, None),
        P(),
        P(both, None),
        P(both, None),
    )
    out_specs = (P(both, None), P(both, None), P(cols, None), P(rows, cols, None))
    return jax.shard_map(shards, mesh=fine, in_specs=in_specs, out_specs=out_specs, check_vma=False)
```

```python
import math

import jax
import jax.numpy as jnp
from jax import lax
from jax.experimental import pallas as pl
from jax.experimental.pallas import tpu as pltpu
from jax.sharding import Mesh
from jax.sharding import PartitionSpec as P

HEADS = 8
HD = 128
TOK = 256
SEGS = 8
TILE = 128
TILES = TOK // TILE
TROWS = TILE * HEADS
ROWS = TOK * HEADS
STATS = TILES * HEADS * 8
PARTS = 3
ROOT_SH = 64
BR_SH = 32
NY = 4
NZ = 4
KB = NY * NZ * BR_SH
SCALE = HD ** (-0.5)
LOG2E = math.log2(math.e)
BIG = 1e30
BF = jnp.bfloat16
F32 = jnp.float32
VMEM = pl.BlockSpec(memory_space=pltpu.VMEM)
HBM = pl.BlockSpec(memory_space=pltpu.HBM)
SMEM = pl.BlockSpec(memory_space=pltpu.SMEM)
PARAMS = pltpu.CompilerParams(vmem_limit_bytes=20 << 20)


def dot(a, b, ca, cb):
    return lax.dot_general(a, b, (((ca,), (cb,)), ((), ())), preferred_element_type=F32)


def split(rows):
    parts = []
    for _ in range(PARTS):
        parts.append(rows.astype(BF))
        rows = rows - parts[-1].astype(F32)
    return parts


def move(rows, onehot):
    return [dot(part, onehot, 1, 1) for part in split(rows)]


def read_stats(qg_ref, stat_ref):
    for t in range(TILES):
        terms = []
        for j in range(4):
            pair = qg_ref[pl.ds(2 * ROWS + (t * 4 + j) * 16, 16), :].astype(F32)
            terms += [pair[:HEADS], pair[HEADS:]]
        norm = (terms[0] + terms[1]) + terms[2]
        delta = (terms[3] + terms[4]) + terms[5]
        norm0 = jnp.where(terms[6] < 0.5, norm, BIG)
        norm1 = jnp.where(terms[6] < 0.5, BIG, norm)
        for h in range(HEADS):
            at = pl.ds((t * HEADS + h) * TILE, TILE)
            for r, value in enumerate((norm, norm0, norm1, delta)):
                stat_ref[r : r + 1, at] = value[h : h + 1]


def pair_terms(keys, values, q, g, norm, delta, mask=None):
    weight = jnp.exp2(dot(keys, q, 1, 1) * (SCALE * LOG2E) - norm)
    if mask is not None:
        weight = jnp.where(mask, weight, 0.0)
    dscore = weight * (dot(values, g, 1, 1) - delta)
    return weight.astype(BF), dscore.astype(BF)


def prepare_kernel(
    seg_branch, q_hbm, o_hbm, g_hbm, norm_ref, leaf_ref, seg_ref,
    qg_ref, onehot_ref, grad_ref, dq_ref, q_ref, o_ref, g_ref, stat_ref, sems,
):
    copies = [
        pltpu.make_async_copy(source, target, sems.at[i])
        for i, (source, target) in enumerate(((q_hbm, q_ref), (g_hbm, g_ref), (o_hbm, o_ref)))
    ]
    for copy in copies:
        copy.start()
    segment = seg_ref[...]
    lane = lax.broadcasted_iota(jnp.int32, (1, TOK), 1)
    branch = jnp.zeros((1, TOK), jnp.int32)
    first = jnp.zeros((1, TOK), jnp.int32)
    for s in range(SEGS):
        here = segment == s
        branch = jnp.where(here, seg_branch[0, s], branch)
        ahead = jnp.sum((segment < s).astype(F32), axis=1, keepdims=True).astype(jnp.int32)
        first = jnp.where(here, ahead, first)
    zero_branch = (branch == 0).astype(F32)
    row = lax.broadcasted_iota(jnp.int32, (TOK, TOK), 0)
    col = lax.broadcasted_iota(jnp.int32, (TOK, TOK), 1)
    before = (row < col).astype(F32).astype(BF)
    count = dot(jnp.broadcast_to(zero_branch, (8, TOK)).astype(BF), before, 1, 0)[:1].astype(jnp.int32)
    zeros = jnp.sum(zero_branch, axis=1, keepdims=True).astype(jnp.int32)
    rank = jnp.where(branch == 0, count, zeros + lane - count)
    onehot = (row == rank).astype(F32).astype(BF)
    onehot_ref[...] = onehot

    for i, source in enumerate((q_ref, g_ref)):
        copies[i].wait()
        for h in range(HEADS):
            moved = dot(onehot, source[:, h * HD : (h + 1) * HD], 1, 0).astype(BF)
            for t in range(TILES):
                qg_ref[pl.ds(i * ROWS + (t * HEADS + h) * TILE, TILE), :] = moved[t * TILE : (t + 1) * TILE]
    copies[2].wait()

    columns = []
    for h in range(HEADS):
        at = slice(h * HD, (h + 1) * HD)
        columns.append(
            jnp.sum(g_ref[:, at].astype(F32) * o_ref[:, at].astype(F32), axis=1, keepdims=True)
        )
    delta = move(jnp.concatenate(columns, axis=1).T, onehot)
    norm = move(norm_ref[...] * LOG2E, onehot)
    place = jnp.concatenate([lane, first, branch, lane, lane, lane, lane, lane], axis=0)
    place = dot(place.astype(F32).astype(BF), onehot, 1, 1)
    flag = jnp.broadcast_to(place[2:3], (HEADS, TOK))
    terms = norm + delta + [flag, flag]
    for t in range(TILES):
        tok = slice(t * TILE, (t + 1) * TILE)
        for j in range(4):
            pair = jnp.concatenate([terms[2 * j][:, tok], terms[2 * j + 1][:, tok]], axis=0)
            qg_ref[pl.ds(2 * ROWS + (t * 4 + j) * 16, 16), :] = pair.astype(BF)
    read_stats(qg_ref, stat_ref)
    place = place.astype(jnp.int32)

    keys = leaf_ref[:, :HD]
    values = leaf_ref[:, HD:]
    keys_t = keys.T
    slot = lax.broadcasted_iota(jnp.int32, (TOK, TILE), 0)
    dkey = jnp.zeros((TOK, HD), F32)
    dvalue = jnp.zeros((TOK, HD), F32)
    for t in range(TILES):
        tok = slice(t * TILE, (t + 1) * TILE)
        mask = ((slot >= place[1:2, tok]) & (slot <= place[0:1, tok])).astype(F32)
        mask = jnp.concatenate([mask] * HEADS, axis=1) > 0.0
        at = pl.ds(t * TROWS, TROWS)
        q = qg_ref[at, :]
        g = qg_ref[pl.ds(ROWS + t * TROWS, TROWS), :]
        weight, dscore = pair_terms(keys, values, q, g, stat_ref[0:1, at], stat_ref[3:4, at], mask)
        dkey += dot(dscore, q, 1, 0)
        dvalue += dot(weight, g, 1, 0)
        dq_ref[:, at] = dot(keys_t, dscore, 1, 0)
    grad_ref[:, :HD] = dkey * SCALE
    grad_ref[:, HD:] = dvalue


def pack_kernel(z0, z1, z2, z3, root_ref, branch_ref):
    for i, piece in enumerate((z0, z1, z2, z3)):
        at = pl.ds(i * ROOT_SH, ROOT_SH)
        root_ref[at, :] = piece[:ROOT_SH, :]
        branch_ref[at, :] = piece[ROOT_SH:, :]


def sweep(kv_ref, sources, norm_row, grads):
    keys = kv_ref[:, :HD]
    values = kv_ref[:, HD:]
    keys_t = keys.T
    for qg_ref, stat_ref, dq_ref in sources:

        def visit(t, carry):
            at = pl.ds(pl.multiple_of(t * TROWS, TROWS), TROWS)
            g_at = pl.ds(pl.multiple_of(ROWS + t * TROWS, TROWS), TROWS)
            norm = stat_ref[norm_row : norm_row + 1, at]

            def work():
                q = qg_ref[at, :]
                g = qg_ref[g_at, :]
                weight, dscore = pair_terms(keys, values, q, g, norm, stat_ref[3:4, at])
                grads[:, :HD] += dot(dscore, q, 1, 0)
                grads[:, HD:] += dot(weight, g, 1, 0)
                dq_ref[:, at] += dot(keys_t, dscore, 1, 0)

            if norm_row == 0:
                work()
            else:
                pl.when(jnp.min(norm) < 0.5 * BIG)(work)
            return carry

        lax.fori_loop(0, TILES, visit, 0)


def root_kernel(kv0, kv1, kv2, kv3, qg0, qg1, dq0, dq1, to0, to1, to2, to3, kv_ref, total, s0, s1):
    dq0[...] = jnp.zeros_like(dq0)
    dq1[...] = jnp.zeros_like(dq1)
    read_stats(qg0, s0)
    read_stats(qg1, s1)
    sources = ((qg0, s0, dq0), (qg1, s1, dq1))
    pieces, targets = (kv0, kv1, kv2, kv3), (to0, to1, to2, to3)
    each = NZ * ROOT_SH
    for dy in range(NY):
        kv_ref[pl.ds(dy * each, each), :] = pieces[dy][...]
    total[...] = jnp.zeros_like(total)
    sweep(kv_ref, sources, 0, total)
    for dy in range(NY):
        at = pl.ds(dy * each, each)
        targets[dy][:, :HD] = (total[at, :HD] * SCALE).astype(BF)
        targets[dy][:, HD:] = total[at, HD:].astype(BF)


def live_slots(place, lengths, b, dy, dz):
    y = lax.rem(place[0] + dy, NY)
    z = lax.rem(place[1] + dz, NZ)
    start = ((y * NZ + z) * 2 + place[2]) * BR_SH
    return lax.broadcasted_iota(jnp.int32, (BR_SH, 1), 0) + start < lengths[place[3] + b]


def branch_other_kernel(place, lengths, kv0, kv1, kv2, kv3, qg_ref, dq_in, dq_ref, kv_ref, total, stat_ref):
    read_stats(qg_ref, stat_ref)
    dq_ref[...] = dq_in[...]
    total[...] = jnp.zeros_like(total)
    for b in range(2):
        for dy, piece in enumerate((kv0, kv1, kv2, kv3)):
            for dz in range(NZ):
                rows = piece[pl.ds((dz * 2 + b) * BR_SH, BR_SH), :].astype(F32)
                at = pl.ds(b * KB + (dy * NZ + dz) * BR_SH, BR_SH)
                kv_ref[at, :] = jnp.where(live_slots(place, lengths, b, dy, dz), rows, 0.0).astype(BF)
        at = pl.ds(b * KB, KB)
        sweep(kv_ref.at[at, :], ((qg_ref, stat_ref, dq_ref),), 1 + b, total.at[at, :])


def branch_own_kernel(
    place, lengths, kv_ref, total_in, qg_ref, dq_in, dq_ref, to0, to1, to2, to3, total, stat_ref
):
    read_stats(qg_ref, stat_ref)
    dq_ref[...] = dq_in[...]
    for b in range(2):
        whole = pl.ds(b * KB, KB)
        total[...] = total_in[whole, :]
        sweep(kv_ref.at[whole, :], ((qg_ref, stat_ref, dq_ref),), 1 + b, total)
        for dy, target in enumerate((to0, to1, to2, to3)):
            for dz in range(NZ):
                ok = live_slots(place, lengths, b, dy, dz)
                at = pl.ds((dy * NZ + dz) * BR_SH, BR_SH)
                to = pl.ds((dz * 2 + b) * BR_SH, BR_SH)
                target[to, :HD] = jnp.where(ok, total[at, :HD] * SCALE, 0.0).astype(BF)
                target[to, HD:] = jnp.where(ok, total[at, HD:], 0.0).astype(BF)


def finish_kernel(onehot_ref, leaf, mine, other, out_ref):
    for h in range(HEADS):
        parts = []
        for t in range(TILES):
            at = pl.ds((t * HEADS + h) * TILE, TILE)
            parts.append((((leaf[:, at] + mine[:, at] + other[:, at]) * SCALE).T).astype(BF))
        column = jnp.concatenate(parts, axis=0)
        out_ref[:, h * HD : (h + 1) * HD] = dot(onehot_ref[...], column, 0, 0).astype(BF)


def shape(dims, dtype):
    return jax.ShapeDtypeStruct(dims, dtype)


def shift(value, axis, size, by):
    return lax.ppermute(value, axis, [(i, (i + by) % size) for i in range(size)])


def gather(value, axis, size):
    return [value] + [shift(value, axis, size, -k) for k in range(1, size)]


def exchange(blocks, axis, size):
    return [blocks[0]] + [shift(blocks[k], axis, size, k) for k in range(1, size)]


def added(terms):
    return sum(term.astype(F32) for term in terms[1:]) + terms[0].astype(F32)


def shards(
    queries, attn_out, out_grad, log_norm, leaf_kv, root_kv, branch_kv, branch_len, segment_ids, segment_branch
):
    first_branch = (lax.axis_index("zl") * 4 + lax.axis_index("x")) * 2
    place = jnp.stack([lax.axis_index("y"), lax.axis_index("zh"), lax.axis_index("c"), first_branch]).astype(jnp.int32)

    shard = jnp.concatenate([root_kv, branch_kv.reshape(2 * BR_SH, 2 * HD)], axis=0)
    block = shape((NZ * ROOT_SH, 2 * HD), BF)
    stats = pltpu.VMEM((4, ROWS), F32)

    qg0, onehot, leaf_grad, dq_leaf = pl.pallas_call(
        prepare_kernel,
        out_shape=(
            shape((2 * ROWS + STATS, HD), BF),
            shape((TOK, TOK), BF),
            shape((TOK, 2 * HD), F32),
            shape((HD, ROWS), F32),
        ),
        in_specs=[SMEM] + [HBM] * 3 + [VMEM] * 3,
        out_specs=(VMEM,) * 4,
        scratch_shapes=[pltpu.VMEM((TOK, HEADS * HD), BF)] * 3 + [stats, pltpu.SemaphoreType.DMA((3,))],
        compiler_params=PARAMS,
        cost_estimate=pl.CostEstimate(flops=4_000_000_000, bytes_accessed=5_000_000, transcendentals=0),
        name="prepare",
    )(segment_branch, *(pltpu.with_memory_space_constraint(x, pltpu.HBM) for x in (queries, attn_out, out_grad)), log_norm.T, leaf_kv, segment_ids)
    pieces, qg0 = lax.optimization_barrier((gather(shard, "zh", NZ), qg0))
    root_z, branch_z = pl.pallas_call(
        pack_kernel,
        out_shape=(block, block),
        in_specs=[VMEM] * 4,
        out_specs=(VMEM,) * 2,
        compiler_params=PARAMS,
        cost_estimate=pl.CostEstimate(flops=0, bytes_accessed=600_000, transcendentals=0),
        name="pack",
    )(*pieces)
    roots = gather(root_z, "y", NY)
    branches = gather(branch_z, "y", NY)
    qg1 = shift(qg0, "c", 2, 1)
    dq_shape = shape((HD, ROWS), F32)


    scratch = [pltpu.VMEM((2 * KB, 2 * HD), BF), pltpu.VMEM((2 * KB, 2 * HD), F32)]

    dq0, dq1, *root_terms = pl.pallas_call(
        root_kernel,
        out_shape=(dq_shape, dq_shape, block, block, block, block),
        in_specs=[VMEM] * 6,
        out_specs=(VMEM,) * 6,
        scratch_shapes=scratch + [stats, stats],
        compiler_params=PARAMS,
        cost_estimate=pl.CostEstimate(flops=10_000_000_000, bytes_accessed=8_000_000, transcendentals=0),
        name="root",
    )(*roots, qg0, qg1)
    root_y = exchange(root_terms, "y", NY)

    branch_cost = pl.CostEstimate(flops=4_500_000_000, bytes_accessed=5_000_000, transcendentals=0)
    dq1, branch_kv_all, branch_total = pl.pallas_call(
        branch_other_kernel,
        out_shape=(dq_shape, shape((2 * KB, 2 * HD), BF), shape((2 * KB, 2 * HD), F32)),
        in_specs=[SMEM] * 2 + [VMEM] * 6,
        out_specs=(VMEM,) * 3,
        scratch_shapes=[stats],
        input_output_aliases={7: 0},
        compiler_params=PARAMS,
        cost_estimate=branch_cost,
        name="branch_other",
    )(place, branch_len, *branches, qg1, dq1)
    root_y, dq1, branch_total = lax.optimization_barrier((root_y, dq1, branch_total))
    other = shift(dq1, "c", 2, 1)
    root_y = added(root_y).astype(BF).reshape(NZ, ROOT_SH, 2 * HD)
    root_z = exchange([root_y[k] for k in range(NZ)], "zh", NZ)

    dq0, *branch_terms = pl.pallas_call(
        branch_own_kernel,
        out_shape=(dq_shape, block, block, block, block),
        in_specs=[SMEM] * 2 + [VMEM] * 4,
        out_specs=(VMEM,) * 5,
        scratch_shapes=[pltpu.VMEM((KB, 2 * HD), F32), stats],
        input_output_aliases={5: 0},
        compiler_params=PARAMS,
        cost_estimate=branch_cost,
        name="branch_own",
    )(place, branch_len, branch_kv_all, branch_total, qg0, dq0)
    root_z, other, branch_terms, dq0 = lax.optimization_barrier((root_z, other, branch_terms, dq0))

    branch_y = exchange(branch_terms, "y", NY)
    query_grad = pl.pallas_call(
        finish_kernel,
        out_shape=shape((TOK, HEADS * HD), BF),
        in_specs=[VMEM] * 4,
        out_specs=VMEM,
        compiler_params=PARAMS,
        cost_estimate=pl.CostEstimate(flops=200_000_000, bytes_accessed=3_000_000, transcendentals=0),
        name="finish",
    )(onehot, dq_leaf, dq0, other)
    root_part = added(root_z)
    pair = lax.ppermute(root_part, "x", [(0, 1), (1, 0), (2, 3), (3, 2)])
    pair, query_grad = lax.optimization_barrier((pair, query_grad))
    root_part = root_part + pair
    pair = lax.ppermute(root_part, "x", [(0, 3), (3, 0), (1, 2), (2, 1)])
    branch_y = added(branch_y).astype(BF).reshape(NZ, 2, BR_SH, 2 * HD)
    branch_z = exchange([branch_y[k] for k in range(NZ)], "zh", NZ)
    root_part = root_part + pair
    root_one = root_part + shift(root_part, "zl", 2, 1)
    branch_one = added(branch_z)
    return query_grad, leaf_grad, root_one, branch_one


def solution(mesh):
    fine = Mesh(mesh.devices.reshape(2, 4, NY, NZ, 2), ("zl", "x", "y", "zh", "c"))
    rows, cols = ("zl", "x"), ("y", "zh", "c")
    both = rows + cols
    in_specs = (
        P(both, None),
        P(both, None),
        P(both, None),
        P(both, None),
        P(both, None),
        P(cols, None),
        P(rows, cols, None),
        P(),
        P(both, None),
        P(both, None),
    )
    out_specs = (P(both, None), P(both, None), P(cols, None), P(rows, cols, None))
    return jax.shard_map(shards, mesh=fine, in_specs=in_specs, out_specs=out_specs, check_vma=False)
```

```python
import math

import jax
import jax.numpy as jnp
from jax import lax
from jax.experimental import pallas as pl
from jax.experimental.pallas import tpu as pltpu
from jax.sharding import Mesh
from jax.sharding import PartitionSpec as P

HEADS = 8
HD = 128
TOK = 256
SEGS = 8
TILE = 128
TILES = TOK // TILE
TROWS = TILE * HEADS
ROWS = TOK * HEADS
STATS = TILES * HEADS * 8
PARTS = 3
ROOT_SH = 64
BR_SH = 32
NY = 4
NZ = 4
KB = NY * NZ * BR_SH
SCALE = HD ** (-0.5)
LOG2E = math.log2(math.e)
BIG = 1e30
BF = jnp.bfloat16
F32 = jnp.float32
VMEM = pl.BlockSpec(memory_space=pltpu.VMEM)
HBM = pl.BlockSpec(memory_space=pltpu.HBM)
SMEM = pl.BlockSpec(memory_space=pltpu.SMEM)
PARAMS = pltpu.CompilerParams(vmem_limit_bytes=20 << 20)


def dot(a, b, ca, cb):
    return lax.dot_general(a, b, (((ca,), (cb,)), ((), ())), preferred_element_type=F32)


def split(rows):
    parts = []
    for _ in range(PARTS):
        parts.append(rows.astype(BF))
        rows = rows - parts[-1].astype(F32)
    return parts


def move(rows, onehot):
    return [dot(part, onehot, 1, 1) for part in split(rows)]


def read_stats(qg_ref, stat_ref):
    for t in range(TILES):
        terms = []
        for j in range(4):
            pair = qg_ref[pl.ds(2 * ROWS + (t * 4 + j) * 16, 16), :].astype(F32)
            terms += [pair[:HEADS], pair[HEADS:]]
        norm = (terms[0] + terms[1]) + terms[2]
        delta = (terms[3] + terms[4]) + terms[5]
        norm0 = jnp.where(terms[6] < 0.5, norm, BIG)
        norm1 = jnp.where(terms[6] < 0.5, BIG, norm)
        for h in range(HEADS):
            at = pl.ds((t * HEADS + h) * TILE, TILE)
            for r, value in enumerate((norm, norm0, norm1, delta)):
                stat_ref[r : r + 1, at] = value[h : h + 1]


def pair_terms(keys, values, q, g, norm, delta, mask=None):
    weight = jnp.exp2(dot(keys, q, 1, 1) * (SCALE * LOG2E) - norm)
    if mask is not None:
        weight = jnp.where(mask, weight, 0.0)
    dscore = weight * (dot(values, g, 1, 1) - delta)
    return weight.astype(BF), dscore.astype(BF)


def prepare_kernel(
    seg_branch, q_hbm, o_hbm, g_hbm, leaf_hbm, norm_ref, seg_ref,
    qg_ref, onehot_ref, grad_ref, dq_ref, q_ref, o_ref, g_ref, leaf_ref, stat_ref, sems,
):
    copies = [
        pltpu.make_async_copy(source, target, sems.at[i])
        for i, (source, target) in enumerate(
            ((q_hbm, q_ref), (g_hbm, g_ref), (o_hbm, o_ref), (leaf_hbm, leaf_ref))
        )
    ]
    for copy in copies:
        copy.start()
    segment = seg_ref[...]
    lane = lax.broadcasted_iota(jnp.int32, (1, TOK), 1)
    branch = jnp.zeros((1, TOK), jnp.int32)
    first = jnp.zeros((1, TOK), jnp.int32)
    for s in range(SEGS):
        here = segment == s
        branch = jnp.where(here, seg_branch[0, s], branch)
        ahead = jnp.sum((segment < s).astype(F32), axis=1, keepdims=True).astype(jnp.int32)
        first = jnp.where(here, ahead, first)
    zero_branch = (branch == 0).astype(F32)
    row = lax.broadcasted_iota(jnp.int32, (TOK, TOK), 0)
    col = lax.broadcasted_iota(jnp.int32, (TOK, TOK), 1)
    before = (row < col).astype(F32).astype(BF)
    count = dot(jnp.broadcast_to(zero_branch, (8, TOK)).astype(BF), before, 1, 0)[:1].astype(jnp.int32)
    zeros = jnp.sum(zero_branch, axis=1, keepdims=True).astype(jnp.int32)
    rank = jnp.where(branch == 0, count, zeros + lane - count)
    onehot = (row == rank).astype(F32).astype(BF)
    onehot_ref[...] = onehot

    for i, source in enumerate((q_ref, g_ref)):
        copies[i].wait()
        for h in range(HEADS):
            moved = dot(onehot, source[:, h * HD : (h + 1) * HD], 1, 0).astype(BF)
            for t in range(TILES):
                qg_ref[pl.ds(i * ROWS + (t * HEADS + h) * TILE, TILE), :] = moved[t * TILE : (t + 1) * TILE]
    copies[2].wait()

    columns = []
    for h in range(HEADS):
        at = slice(h * HD, (h + 1) * HD)
        columns.append(
            jnp.sum(g_ref[:, at].astype(F32) * o_ref[:, at].astype(F32), axis=1, keepdims=True)
        )
    delta = move(jnp.concatenate(columns, axis=1).T, onehot)
    norm = move(norm_ref[...] * LOG2E, onehot)
    place = jnp.concatenate([lane, first, branch, lane, lane, lane, lane, lane], axis=0)
    place = dot(place.astype(F32).astype(BF), onehot, 1, 1)
    flag = jnp.broadcast_to(place[2:3], (HEADS, TOK))
    terms = norm + delta + [flag, flag]
    for t in range(TILES):
        tok = slice(t * TILE, (t + 1) * TILE)
        for j in range(4):
            pair = jnp.concatenate([terms[2 * j][:, tok], terms[2 * j + 1][:, tok]], axis=0)
            qg_ref[pl.ds(2 * ROWS + (t * 4 + j) * 16, 16), :] = pair.astype(BF)
    read_stats(qg_ref, stat_ref)
    place = place.astype(jnp.int32)

    copies[3].wait()
    keys = leaf_ref[:, :HD]
    values = leaf_ref[:, HD:]
    keys_t = keys.T
    slot = lax.broadcasted_iota(jnp.int32, (TOK, TILE), 0)
    dkey = jnp.zeros((TOK, HD), F32)
    dvalue = jnp.zeros((TOK, HD), F32)
    for t in range(TILES):
        tok = slice(t * TILE, (t + 1) * TILE)
        mask = ((slot >= place[1:2, tok]) & (slot <= place[0:1, tok])).astype(F32)
        mask = jnp.concatenate([mask] * HEADS, axis=1) > 0.0
        at = pl.ds(t * TROWS, TROWS)
        q = qg_ref[at, :]
        g = qg_ref[pl.ds(ROWS + t * TROWS, TROWS), :]
        weight, dscore = pair_terms(keys, values, q, g, stat_ref[0:1, at], stat_ref[3:4, at], mask)
        dkey += dot(dscore, q, 1, 0)
        dvalue += dot(weight, g, 1, 0)
        dq_ref[:, at] = dot(keys_t, dscore, 1, 0)
    grad_ref[:, :HD] = dkey * SCALE
    grad_ref[:, HD:] = dvalue


def pack_kernel(z0, z1, z2, z3, root_ref, branch_ref):
    for i, piece in enumerate((z0, z1, z2, z3)):
        at = pl.ds(i * ROOT_SH, ROOT_SH)
        root_ref[at, :] = piece[:ROOT_SH, :]
        branch_ref[at, :] = piece[ROOT_SH:, :]


def sweep(kv_ref, sources, norm_row, grads):
    keys = kv_ref[:, :HD]
    values = kv_ref[:, HD:]
    keys_t = keys.T
    for qg_ref, stat_ref, dq_ref in sources:

        def visit(t, carry):
            at = pl.ds(pl.multiple_of(t * TROWS, TROWS), TROWS)
            g_at = pl.ds(pl.multiple_of(ROWS + t * TROWS, TROWS), TROWS)
            norm = stat_ref[norm_row : norm_row + 1, at]

            def work():
                q = qg_ref[at, :]
                g = qg_ref[g_at, :]
                weight, dscore = pair_terms(keys, values, q, g, norm, stat_ref[3:4, at])
                grads[:, :HD] += dot(dscore, q, 1, 0)
                grads[:, HD:] += dot(weight, g, 1, 0)
                dq_ref[:, at] += dot(keys_t, dscore, 1, 0)

            if norm_row == 0:
                work()
            else:
                pl.when(jnp.min(norm) < 0.5 * BIG)(work)
            return carry

        lax.fori_loop(0, TILES, visit, 0)


def root_kernel(kv0, kv1, kv2, kv3, qg0, qg1, dq0, dq1, to0, to1, to2, to3, kv_ref, total, s0, s1):
    dq0[...] = jnp.zeros_like(dq0)
    dq1[...] = jnp.zeros_like(dq1)
    read_stats(qg0, s0)
    read_stats(qg1, s1)
    sources = ((qg0, s0, dq0), (qg1, s1, dq1))
    pieces, targets = (kv0, kv1, kv2, kv3), (to0, to1, to2, to3)
    each = NZ * ROOT_SH
    for dy in range(NY):
        kv_ref[pl.ds(dy * each, each), :] = pieces[dy][...]
    total[...] = jnp.zeros_like(total)
    sweep(kv_ref, sources, 0, total)
    for dy in range(NY):
        at = pl.ds(dy * each, each)
        targets[dy][:, :HD] = (total[at, :HD] * SCALE).astype(BF)
        targets[dy][:, HD:] = total[at, HD:].astype(BF)


def live_slots(place, lengths, b, dy, dz):
    y = lax.rem(place[0] + dy, NY)
    z = lax.rem(place[1] + dz, NZ)
    start = ((y * NZ + z) * 2 + place[2]) * BR_SH
    return lax.broadcasted_iota(jnp.int32, (BR_SH, 1), 0) + start < lengths[place[3] + b]


def branch_other_kernel(place, lengths, kv0, kv1, kv2, kv3, qg_ref, dq_in, dq_ref, kv_ref, total, stat_ref):
    read_stats(qg_ref, stat_ref)
    dq_ref[...] = dq_in[...]
    total[...] = jnp.zeros_like(total)
    for b in range(2):
        for dy, piece in enumerate((kv0, kv1, kv2, kv3)):
            for dz in range(NZ):
                rows = piece[pl.ds((dz * 2 + b) * BR_SH, BR_SH), :].astype(F32)
                at = pl.ds(b * KB + (dy * NZ + dz) * BR_SH, BR_SH)
                kv_ref[at, :] = jnp.where(live_slots(place, lengths, b, dy, dz), rows, 0.0).astype(BF)
        at = pl.ds(b * KB, KB)
        sweep(kv_ref.at[at, :], ((qg_ref, stat_ref, dq_ref),), 1 + b, total.at[at, :])


def branch_own_kernel(
    place, lengths, kv_ref, total_in, qg_ref, dq_in, dq_ref, to0, to1, to2, to3, total, stat_ref
):
    read_stats(qg_ref, stat_ref)
    dq_ref[...] = dq_in[...]
    for b in range(2):
        whole = pl.ds(b * KB, KB)
        total[...] = total_in[whole, :]
        sweep(kv_ref.at[whole, :], ((qg_ref, stat_ref, dq_ref),), 1 + b, total)
        for dy, target in enumerate((to0, to1, to2, to3)):
            for dz in range(NZ):
                ok = live_slots(place, lengths, b, dy, dz)
                at = pl.ds((dy * NZ + dz) * BR_SH, BR_SH)
                to = pl.ds((dz * 2 + b) * BR_SH, BR_SH)
                target[to, :HD] = jnp.where(ok, total[at, :HD] * SCALE, 0.0).astype(BF)
                target[to, HD:] = jnp.where(ok, total[at, HD:], 0.0).astype(BF)


def finish_kernel(onehot_ref, leaf, mine, other, out_ref):
    for h in range(HEADS):
        parts = []
        for t in range(TILES):
            at = pl.ds((t * HEADS + h) * TILE, TILE)
            parts.append((((leaf[:, at] + mine[:, at] + other[:, at]) * SCALE).T).astype(BF))
        column = jnp.concatenate(parts, axis=0)
        out_ref[:, h * HD : (h + 1) * HD] = dot(onehot_ref[...], column, 0, 0).astype(BF)


def in_hbm(value):
    return pltpu.with_memory_space_constraint(value, pltpu.HBM)


def shape(dims, dtype):
    return jax.ShapeDtypeStruct(dims, dtype)


def shift(value, axis, size, by):
    return lax.ppermute(value, axis, [(i, (i + by) % size) for i in range(size)])


def gather(value, axis, size):
    return [value] + [shift(value, axis, size, -k) for k in range(1, size)]


def exchange(blocks, axis, size):
    return [blocks[0]] + [shift(blocks[k], axis, size, k) for k in range(1, size)]


def added(terms):
    return sum(term.astype(F32) for term in terms[1:]) + terms[0].astype(F32)


def shards(
    queries, attn_out, out_grad, log_norm, leaf_kv, root_kv, branch_kv, branch_len, segment_ids, segment_branch
):
    first_branch = (lax.axis_index("zl") * 4 + lax.axis_index("x")) * 2
    place = jnp.stack([lax.axis_index("y"), lax.axis_index("zh"), lax.axis_index("c"), first_branch]).astype(jnp.int32)

    shard = jnp.concatenate([root_kv, branch_kv.reshape(2 * BR_SH, 2 * HD)], axis=0)
    block = shape((NZ * ROOT_SH, 2 * HD), BF)
    stats = pltpu.VMEM((4, ROWS), F32)

    qg0, onehot, leaf_grad, dq_leaf = pl.pallas_call(
        prepare_kernel,
        out_shape=(
            shape((2 * ROWS + STATS, HD), BF),
            shape((TOK, TOK), BF),
            shape((TOK, 2 * HD), F32),
            shape((HD, ROWS), F32),
        ),
        in_specs=[SMEM] + [HBM] * 4 + [VMEM] * 2,
        out_specs=(VMEM,) * 4,
        scratch_shapes=[pltpu.VMEM((TOK, HEADS * HD), BF)] * 3
        + [pltpu.VMEM((TOK, 2 * HD), BF), stats, pltpu.SemaphoreType.DMA((4,))],
        compiler_params=PARAMS,
        cost_estimate=pl.CostEstimate(flops=4_000_000_000, bytes_accessed=5_000_000, transcendentals=0),
        name="prepare",
    )(in_hbm(segment_branch), *(in_hbm(x) for x in (queries, attn_out, out_grad, leaf_kv, log_norm.T, segment_ids)))
    pieces, qg0 = lax.optimization_barrier((gather(shard, "zh", NZ), qg0))
    root_z, branch_z = pl.pallas_call(
        pack_kernel,
        out_shape=(block, block),
        in_specs=[VMEM] * 4,
        out_specs=(VMEM,) * 2,
        compiler_params=PARAMS,
        cost_estimate=pl.CostEstimate(flops=0, bytes_accessed=600_000, transcendentals=0),
        name="pack",
    )(*pieces)
    roots = gather(root_z, "y", NY)
    branches = gather(branch_z, "y", NY)
    qg1 = shift(qg0, "c", 2, 1)
    dq_shape = shape((HD, ROWS), F32)


    scratch = [pltpu.VMEM((2 * KB, 2 * HD), BF), pltpu.VMEM((2 * KB, 2 * HD), F32)]

    dq0, dq1, *root_terms = pl.pallas_call(
        root_kernel,
        out_shape=(dq_shape, dq_shape, block, block, block, block),
        in_specs=[VMEM] * 6,
        out_specs=(VMEM,) * 6,
        scratch_shapes=scratch + [stats, stats],
        compiler_params=PARAMS,
        cost_estimate=pl.CostEstimate(flops=10_000_000_000, bytes_accessed=8_000_000, transcendentals=0),
        name="root",
    )(*roots, qg0, qg1)
    root_y = exchange(root_terms, "y", NY)

    branch_cost = pl.CostEstimate(flops=4_500_000_000, bytes_accessed=5_000_000, transcendentals=0)
    dq1, branch_kv_all, branch_total = pl.pallas_call(
        branch_other_kernel,
        out_shape=(dq_shape, shape((2 * KB, 2 * HD), BF), shape((2 * KB, 2 * HD), F32)),
        in_specs=[SMEM] * 2 + [VMEM] * 6,
        out_specs=(VMEM,) * 3,
        scratch_shapes=[stats],
        input_output_aliases={7: 0},
        compiler_params=PARAMS,
        cost_estimate=branch_cost,
        name="branch_other",
    )(place, branch_len, *branches, qg1, dq1)
    root_y, dq1, branch_total = lax.optimization_barrier((root_y, dq1, branch_total))
    other = shift(dq1, "c", 2, 1)
    root_y = added(root_y).astype(BF).reshape(NZ, ROOT_SH, 2 * HD)
    root_z = exchange([root_y[k] for k in range(NZ)], "zh", NZ)

    dq0, *branch_terms = pl.pallas_call(
        branch_own_kernel,
        out_shape=(dq_shape, block, block, block, block),
        in_specs=[SMEM] * 2 + [VMEM] * 4,
        out_specs=(VMEM,) * 5,
        scratch_shapes=[pltpu.VMEM((KB, 2 * HD), F32), stats],
        input_output_aliases={5: 0},
        compiler_params=PARAMS,
        cost_estimate=branch_cost,
        name="branch_own",
    )(place, branch_len, branch_kv_all, branch_total, qg0, dq0)
    root_z, other, branch_terms, dq0 = lax.optimization_barrier((root_z, other, branch_terms, dq0))

    branch_y = exchange(branch_terms, "y", NY)
    query_grad = pl.pallas_call(
        finish_kernel,
        out_shape=shape((TOK, HEADS * HD), BF),
        in_specs=[VMEM] * 4,
        out_specs=VMEM,
        compiler_params=PARAMS,
        cost_estimate=pl.CostEstimate(flops=200_000_000, bytes_accessed=3_000_000, transcendentals=0),
        name="finish",
    )(onehot, dq_leaf, dq0, other)
    root_part = added(root_z)
    pair = lax.ppermute(root_part, "x", [(0, 1), (1, 0), (2, 3), (3, 2)])
    pair, query_grad = lax.optimization_barrier((pair, query_grad))
    root_part = root_part + pair
    pair = lax.ppermute(root_part, "x", [(0, 3), (3, 0), (1, 2), (2, 1)])
    branch_y = added(branch_y).astype(BF).reshape(NZ, 2, BR_SH, 2 * HD)
    branch_z = exchange([branch_y[k] for k in range(NZ)], "zh", NZ)
    root_part = root_part + pair
    root_one = root_part + shift(root_part, "zl", 2, 1)
    branch_one = added(branch_z)
    return query_grad, leaf_grad, root_one, branch_one


def solution(mesh):
    fine = Mesh(mesh.devices.reshape(2, 4, NY, NZ, 2), ("zl", "x", "y", "zh", "c"))
    rows, cols = ("zl", "x"), ("y", "zh", "c")
    both = rows + cols
    in_specs = (
        P(both, None),
        P(both, None),
        P(both, None),
        P(both, None),
        P(both, None),
        P(cols, None),
        P(rows, cols, None),
        P(),
        P(both, None),
        P(both, None),
    )
    out_specs = (P(both, None), P(both, None), P(cols, None), P(rows, cols, None))
    return jax.shard_map(shards, mesh=fine, in_specs=in_specs, out_specs=out_specs, check_vma=False)
```

```python
import math

import jax
import jax.numpy as jnp
from jax import lax
from jax.experimental import pallas as pl
from jax.experimental.pallas import tpu as pltpu
from jax.sharding import Mesh
from jax.sharding import PartitionSpec as P

HEADS = 8
HD = 128
TOK = 256
SEGS = 8
TILE = 128
TILES = TOK // TILE
TROWS = TILE * HEADS
ROWS = TOK * HEADS
STATS = TILES * HEADS * 8
PARTS = 3
ROOT_SH = 64
BR_SH = 32
NY = 4
NZ = 4
KB = NY * NZ * BR_SH
SCALE = HD ** (-0.5)
LOG2E = math.log2(math.e)
BIG = 1e30
BF = jnp.bfloat16
F32 = jnp.float32
VMEM = pl.BlockSpec(memory_space=pltpu.VMEM)
HBM = pl.BlockSpec(memory_space=pltpu.HBM)
SMEM = pl.BlockSpec(memory_space=pltpu.SMEM)
PARAMS = pltpu.CompilerParams(vmem_limit_bytes=20 << 20)


def dot(a, b, ca, cb):
    return lax.dot_general(a, b, (((ca,), (cb,)), ((), ())), preferred_element_type=F32)


def split(rows):
    parts = []
    for _ in range(PARTS):
        parts.append(rows.astype(BF))
        rows = rows - parts[-1].astype(F32)
    return parts


def move(rows, onehot):
    return [dot(part, onehot, 1, 1) for part in split(rows)]


def read_stats(qg_ref, stat_ref):
    for t in range(TILES):
        terms = []
        for j in range(4):
            pair = qg_ref[pl.ds(2 * ROWS + (t * 4 + j) * 16, 16), :].astype(F32)
            terms += [pair[:HEADS], pair[HEADS:]]
        norm = (terms[0] + terms[1]) + terms[2]
        delta = (terms[3] + terms[4]) + terms[5]
        norm0 = jnp.where(terms[6] < 0.5, norm, BIG)
        norm1 = jnp.where(terms[6] < 0.5, BIG, norm)
        for h in range(HEADS):
            at = pl.ds((t * HEADS + h) * TILE, TILE)
            for r, value in enumerate((norm, norm0, norm1, delta)):
                stat_ref[r : r + 1, at] = value[h : h + 1]


def pair_terms(keys, values, q, g, norm, delta, mask=None):
    weight = jnp.exp2(dot(keys, q, 1, 1) * (SCALE * LOG2E) - norm)
    if mask is not None:
        weight = jnp.where(mask, weight, 0.0)
    dscore = weight * (dot(values, g, 1, 1) - delta)
    return weight.astype(BF), dscore.astype(BF)


def prepare_kernel(
    seg_branch, q_hbm, o_hbm, g_hbm, leaf_hbm, norm_ref, seg_ref,
    qg_ref, onehot_ref, grad_ref, dq_ref, q_ref, o_ref, g_ref, leaf_ref, stat_ref, sems,
):
    copies = [
        pltpu.make_async_copy(source, target, sems.at[i])
        for i, (source, target) in enumerate(
            ((q_hbm, q_ref), (g_hbm, g_ref), (o_hbm, o_ref), (leaf_hbm, leaf_ref))
        )
    ]
    for copy in copies:
        copy.start()
    segment = seg_ref[...]
    lane = lax.broadcasted_iota(jnp.int32, (1, TOK), 1)
    branch = jnp.zeros((1, TOK), jnp.int32)
    first = jnp.zeros((1, TOK), jnp.int32)
    for s in range(SEGS):
        here = segment == s
        branch = jnp.where(here, seg_branch[0, s], branch)
        ahead = jnp.sum((segment < s).astype(F32), axis=1, keepdims=True).astype(jnp.int32)
        first = jnp.where(here, ahead, first)
    zero_branch = (branch == 0).astype(F32)
    row = lax.broadcasted_iota(jnp.int32, (TOK, TOK), 0)
    col = lax.broadcasted_iota(jnp.int32, (TOK, TOK), 1)
    before = (row < col).astype(F32).astype(BF)
    count = dot(jnp.broadcast_to(zero_branch, (8, TOK)).astype(BF), before, 1, 0)[:1].astype(jnp.int32)
    zeros = jnp.sum(zero_branch, axis=1, keepdims=True).astype(jnp.int32)
    rank = jnp.where(branch == 0, count, zeros + lane - count)
    onehot = (row == rank).astype(F32).astype(BF)
    onehot_ref[...] = onehot

    for i, source in enumerate((q_ref, g_ref)):
        copies[i].wait()
        for h in range(HEADS):
            moved = dot(onehot, source[:, h * HD : (h + 1) * HD], 1, 0).astype(BF)
            for t in range(TILES):
                qg_ref[pl.ds(i * ROWS + (t * HEADS + h) * TILE, TILE), :] = moved[t * TILE : (t + 1) * TILE]
    copies[2].wait()

    columns = []
    for h in range(HEADS):
        at = slice(h * HD, (h + 1) * HD)
        columns.append(
            jnp.sum(g_ref[:, at].astype(F32) * o_ref[:, at].astype(F32), axis=1, keepdims=True)
        )
    delta = move(jnp.concatenate(columns, axis=1).T, onehot)
    norm = move(norm_ref[...] * LOG2E, onehot)
    place = jnp.concatenate([lane, first, branch, lane, lane, lane, lane, lane], axis=0)
    place = dot(place.astype(F32).astype(BF), onehot, 1, 1)
    flag = jnp.broadcast_to(place[2:3], (HEADS, TOK))
    terms = norm + delta + [flag, flag]
    for t in range(TILES):
        tok = slice(t * TILE, (t + 1) * TILE)
        for j in range(4):
            pair = jnp.concatenate([terms[2 * j][:, tok], terms[2 * j + 1][:, tok]], axis=0)
            qg_ref[pl.ds(2 * ROWS + (t * 4 + j) * 16, 16), :] = pair.astype(BF)
    read_stats(qg_ref, stat_ref)
    place = place.astype(jnp.int32)

    copies[3].wait()
    keys = leaf_ref[:, :HD]
    values = leaf_ref[:, HD:]
    keys_t = keys.T
    slot = lax.broadcasted_iota(jnp.int32, (TOK, TILE), 0)
    dkey = jnp.zeros((TOK, HD), F32)
    dvalue = jnp.zeros((TOK, HD), F32)
    for t in range(TILES):
        tok = slice(t * TILE, (t + 1) * TILE)
        mask = ((slot >= place[1:2, tok]) & (slot <= place[0:1, tok])).astype(F32)
        mask = jnp.concatenate([mask] * HEADS, axis=1) > 0.0
        at = pl.ds(t * TROWS, TROWS)
        q = qg_ref[at, :]
        g = qg_ref[pl.ds(ROWS + t * TROWS, TROWS), :]
        weight, dscore = pair_terms(keys, values, q, g, stat_ref[0:1, at], stat_ref[3:4, at], mask)
        dkey += dot(dscore, q, 1, 0)
        dvalue += dot(weight, g, 1, 0)
        dq_ref[:, at] = dot(keys_t, dscore, 1, 0)
    grad_ref[:, :HD] = dkey * SCALE
    grad_ref[:, HD:] = dvalue


def pack_kernel(z0, z1, z2, z3, root_ref, branch_ref):
    for i, piece in enumerate((z0, z1, z2, z3)):
        at = pl.ds(i * ROOT_SH, ROOT_SH)
        root_ref[at, :] = piece[:ROOT_SH, :]
        branch_ref[at, :] = piece[ROOT_SH:, :]


def sweep(kv_ref, sources, norm_row, grads):
    keys = kv_ref[:, :HD]
    values = kv_ref[:, HD:]
    keys_t = keys.T
    for qg_ref, stat_ref, dq_ref in sources:

        def visit(t, carry):
            at = pl.ds(pl.multiple_of(t * TROWS, TROWS), TROWS)
            g_at = pl.ds(pl.multiple_of(ROWS + t * TROWS, TROWS), TROWS)
            norm = stat_ref[norm_row : norm_row + 1, at]

            def work():
                q = qg_ref[at, :]
                g = qg_ref[g_at, :]
                weight, dscore = pair_terms(keys, values, q, g, norm, stat_ref[3:4, at])
                grads[:, :HD] += dot(dscore, q, 1, 0)
                grads[:, HD:] += dot(weight, g, 1, 0)
                dq_ref[:, at] += dot(keys_t, dscore, 1, 0)

            if norm_row == 0:
                work()
            else:
                pl.when(jnp.min(norm) < 0.5 * BIG)(work)
            return carry

        lax.fori_loop(0, TILES, visit, 0)


def root_kernel(kv0, kv1, kv2, kv3, qg0, qg1, dq0, dq1, to0, to1, to2, to3, kv_ref, total, s0, s1):
    dq0[...] = jnp.zeros_like(dq0)
    dq1[...] = jnp.zeros_like(dq1)
    read_stats(qg0, s0)
    read_stats(qg1, s1)
    sources = ((qg0, s0, dq0), (qg1, s1, dq1))
    pieces, targets = (kv0, kv1, kv2, kv3), (to0, to1, to2, to3)
    each = NZ * ROOT_SH
    for dy in range(NY):
        kv_ref[pl.ds(dy * each, each), :] = pieces[dy][...]
    total[...] = jnp.zeros_like(total)
    sweep(kv_ref, sources, 0, total)
    for dy in range(NY):
        at = pl.ds(dy * each, each)
        targets[dy][:, :HD] = (total[at, :HD] * SCALE).astype(BF)
        targets[dy][:, HD:] = total[at, HD:].astype(BF)


def live_slots(place, lengths, b, dy, dz):
    y = lax.rem(place[0] + dy, NY)
    z = lax.rem(place[1] + dz, NZ)
    start = ((y * NZ + z) * 2 + place[2]) * BR_SH
    return lax.broadcasted_iota(jnp.int32, (BR_SH, 1), 0) + start < lengths[place[3] + b]


def branch_other_kernel(place, lengths, kv0, kv1, kv2, kv3, qg_ref, dq_in, dq_ref, kv_ref, total, stat_ref):
    read_stats(qg_ref, stat_ref)
    dq_ref[...] = dq_in[...]
    total[...] = jnp.zeros_like(total)
    for b in range(2):
        for dy, piece in enumerate((kv0, kv1, kv2, kv3)):
            for dz in range(NZ):
                rows = piece[pl.ds((dz * 2 + b) * BR_SH, BR_SH), :].astype(F32)
                at = pl.ds(b * KB + (dy * NZ + dz) * BR_SH, BR_SH)
                kv_ref[at, :] = jnp.where(live_slots(place, lengths, b, dy, dz), rows, 0.0).astype(BF)
        at = pl.ds(b * KB, KB)
        sweep(kv_ref.at[at, :], ((qg_ref, stat_ref, dq_ref),), 1 + b, total.at[at, :])


def branch_own_kernel(
    place, lengths, kv_ref, total_in, qg_ref, dq_in, dq_ref, to0, to1, to2, to3, total, stat_ref
):
    read_stats(qg_ref, stat_ref)
    dq_ref[...] = dq_in[...]
    for b in range(2):
        whole = pl.ds(b * KB, KB)
        total[...] = total_in[whole, :]
        sweep(kv_ref.at[whole, :], ((qg_ref, stat_ref, dq_ref),), 1 + b, total)
        for dy, target in enumerate((to0, to1, to2, to3)):
            for dz in range(NZ):
                ok = live_slots(place, lengths, b, dy, dz)
                at = pl.ds((dy * NZ + dz) * BR_SH, BR_SH)
                to = pl.ds((dz * 2 + b) * BR_SH, BR_SH)
                target[to, :HD] = jnp.where(ok, total[at, :HD] * SCALE, 0.0).astype(BF)
                target[to, HD:] = jnp.where(ok, total[at, HD:], 0.0).astype(BF)


def finish_kernel(onehot_ref, leaf, mine, other, out_ref):
    for h in range(HEADS):
        parts = []
        for t in range(TILES):
            at = pl.ds((t * HEADS + h) * TILE, TILE)
            parts.append((((leaf[:, at] + mine[:, at] + other[:, at]) * SCALE).T).astype(BF))
        column = jnp.concatenate(parts, axis=0)
        out_ref[:, h * HD : (h + 1) * HD] = dot(onehot_ref[...], column, 0, 0).astype(BF)


def in_hbm(value):
    return pltpu.with_memory_space_constraint(value, pltpu.HBM)


def shape(dims, dtype):
    return jax.ShapeDtypeStruct(dims, dtype)


def shift(value, axis, size, by):
    return lax.ppermute(value, axis, [(i, (i + by) % size) for i in range(size)])


def gather(value, axis, size):
    return [value] + [shift(value, axis, size, -k) for k in range(1, size)]


def exchange(blocks, axis, size):
    return [blocks[0]] + [shift(blocks[k], axis, size, k) for k in range(1, size)]


def added(terms):
    return sum(term.astype(F32) for term in terms[1:]) + terms[0].astype(F32)


def shards(
    queries, attn_out, out_grad, log_norm, leaf_kv, root_kv, branch_kv, branch_len, segment_ids, segment_branch
):
    first_branch = (lax.axis_index("zl") * 4 + lax.axis_index("x")) * 2
    place = jnp.stack([lax.axis_index("y"), lax.axis_index("zh"), lax.axis_index("c"), first_branch]).astype(jnp.int32)

    shard = jnp.concatenate([root_kv, branch_kv.reshape(2 * BR_SH, 2 * HD)], axis=0)
    block = shape((NZ * ROOT_SH, 2 * HD), BF)
    stats = pltpu.VMEM((4, ROWS), F32)

    qg0, onehot, leaf_grad, dq_leaf = pl.pallas_call(
        prepare_kernel,
        out_shape=(
            shape((2 * ROWS + STATS, HD), BF),
            shape((TOK, TOK), BF),
            shape((TOK, 2 * HD), F32),
            shape((HD, ROWS), F32),
        ),
        in_specs=[SMEM] + [HBM] * 4 + [VMEM] * 2,
        out_specs=(VMEM,) * 4,
        scratch_shapes=[pltpu.VMEM((TOK, HEADS * HD), BF)] * 3
        + [pltpu.VMEM((TOK, 2 * HD), BF), stats, pltpu.SemaphoreType.DMA((4,))],
        compiler_params=PARAMS,
        cost_estimate=pl.CostEstimate(flops=4_000_000_000, bytes_accessed=5_000_000, transcendentals=0),
        name="prepare",
    )(in_hbm(segment_branch), *(in_hbm(x) for x in (queries, attn_out, out_grad, leaf_kv, log_norm.T, segment_ids)))
    pieces, qg0 = lax.optimization_barrier((gather(shard, "zh", NZ), qg0))
    root_z, branch_z = pl.pallas_call(
        pack_kernel,
        out_shape=(block, block),
        in_specs=[VMEM] * 4,
        out_specs=(VMEM,) * 2,
        compiler_params=PARAMS,
        cost_estimate=pl.CostEstimate(flops=0, bytes_accessed=600_000, transcendentals=0),
        name="pack",
    )(*pieces)
    roots = gather(root_z, "y", NY)
    qg1, branch_z = lax.optimization_barrier((shift(qg0, "c", 2, 1), branch_z))
    branches = gather(branch_z, "y", NY)
    dq_shape = shape((HD, ROWS), F32)


    scratch = [pltpu.VMEM((2 * KB, 2 * HD), BF), pltpu.VMEM((2 * KB, 2 * HD), F32)]

    dq0, dq1, *root_terms = pl.pallas_call(
        root_kernel,
        out_shape=(dq_shape, dq_shape, block, block, block, block),
        in_specs=[VMEM] * 6,
        out_specs=(VMEM,) * 6,
        scratch_shapes=scratch + [stats, stats],
        compiler_params=PARAMS,
        cost_estimate=pl.CostEstimate(flops=10_000_000_000, bytes_accessed=8_000_000, transcendentals=0),
        name="root",
    )(*roots, qg0, qg1)
    root_y = exchange(root_terms, "y", NY)

    branch_cost = pl.CostEstimate(flops=4_500_000_000, bytes_accessed=5_000_000, transcendentals=0)
    dq1, branch_kv_all, branch_total = pl.pallas_call(
        branch_other_kernel,
        out_shape=(dq_shape, shape((2 * KB, 2 * HD), BF), shape((2 * KB, 2 * HD), F32)),
        in_specs=[SMEM] * 2 + [VMEM] * 6,
        out_specs=(VMEM,) * 3,
        scratch_shapes=[stats],
        input_output_aliases={7: 0},
        compiler_params=PARAMS,
        cost_estimate=branch_cost,
        name="branch_other",
    )(place, branch_len, *branches, qg1, dq1)
    root_y, dq1, branch_total = lax.optimization_barrier((root_y, dq1, branch_total))
    other = shift(dq1, "c", 2, 1)
    root_y = added(root_y).astype(BF).reshape(NZ, ROOT_SH, 2 * HD)
    root_z = exchange([root_y[k] for k in range(NZ)], "zh", NZ)

    dq0, *branch_terms = pl.pallas_call(
        branch_own_kernel,
        out_shape=(dq_shape, block, block, block, block),
        in_specs=[SMEM] * 2 + [VMEM] * 4,
        out_specs=(VMEM,) * 5,
        scratch_shapes=[pltpu.VMEM((KB, 2 * HD), F32), stats],
        input_output_aliases={5: 0},
        compiler_params=PARAMS,
        cost_estimate=branch_cost,
        name="branch_own",
    )(place, branch_len, branch_kv_all, branch_total, qg0, dq0)
    root_z, other, branch_terms, dq0 = lax.optimization_barrier((root_z, other, branch_terms, dq0))

    branch_y = exchange(branch_terms, "y", NY)
    query_grad = pl.pallas_call(
        finish_kernel,
        out_shape=shape((TOK, HEADS * HD), BF),
        in_specs=[VMEM] * 4,
        out_specs=VMEM,
        compiler_params=PARAMS,
        cost_estimate=pl.CostEstimate(flops=200_000_000, bytes_accessed=3_000_000, transcendentals=0),
        name="finish",
    )(onehot, dq_leaf, dq0, other)
    root_part = added(root_z)
    pair = lax.ppermute(root_part, "x", [(0, 1), (1, 0), (2, 3), (3, 2)])
    pair, query_grad = lax.optimization_barrier((pair, query_grad))
    root_part = root_part + pair
    pair = lax.ppermute(root_part, "x", [(0, 3), (3, 0), (1, 2), (2, 1)])
    branch_y = added(branch_y).astype(BF).reshape(NZ, 2, BR_SH, 2 * HD)
    branch_z = exchange([branch_y[k] for k in range(NZ)], "zh", NZ)
    root_part = root_part + pair
    root_one = root_part + shift(root_part, "zl", 2, 1)
    branch_one = added(branch_z)
    return query_grad, leaf_grad, root_one, branch_one


def solution(mesh):
    fine = Mesh(mesh.devices.reshape(2, 4, NY, NZ, 2), ("zl", "x", "y", "zh", "c"))
    rows, cols = ("zl", "x"), ("y", "zh", "c")
    both = rows + cols
    in_specs = (
        P(both, None),
        P(both, None),
        P(both, None),
        P(both, None),
        P(both, None),
        P(cols, None),
        P(rows, cols, None),
        P(),
        P(both, None),
        P(both, None),
    )
    out_specs = (P(both, None), P(both, None), P(cols, None), P(rows, cols, None))
    return jax.shard_map(shards, mesh=fine, in_specs=in_specs, out_specs=out_specs, check_vma=False)
```
